256 devices in a mesh: seq: 32 (over y, z_hi, core), col: 8 (over x, z_lo).
Axes of the slice: x: 4, y: 4, z: 8 (z_hi: 4, z_lo: 2; z = z_hi * 2 + z_lo), core: 2. Of those that a mesh axis runs over, the one named last changes fastest.
Arguments:
- memory: bfloat16 [4096, 4096], P('col', 'seq'), may hold values from -8 to 8
- query: bfloat16 [8192, 2048], P('seq', 'col'), may hold values from -400 to 400
- out_grad: bfloat16 [8192, 2048], P('seq', 'col'), may hold values from -96 to 96
- w_key: bfloat16 [4096, 2048], P(None, 'col'), may hold values from -0.09375 to 0.09375
- w_value: bfloat16 [4096, 2048], P(None, 'col'), may hold values from -0.09375 to 0.09375
Outputs:
- d_query: bfloat16 [8192, 2048], P('seq', 'col')
- d_memory: bfloat16 [4096, 4096], P('col', 'seq')
The draws below stay inside these ranges and needn't reach their ends.
All inputs are finite; a program needn't handle non-finite values.
Results may differ from the reference program's by a relative error of at most 0.02.
The reference program's roundings to bfloat16 on the way (of `key_rows`, `value_rows`, `weights_low`, `score_grad`, `key_grad` and `value_grad`) count: a program that leaves them out, or rounds other values in their place, can miss the bound.
Values may be sent and summed in bfloat16 or wider, within the bound.
A program may use at most 128 MiB of HBM per device.

```python
import math
import jax
import jax.numpy as jnp
from jax import lax

D = 4096
HD = 64
HEADS = 32
INNER = 2048
SRC = 4096
TGT = 8192


def shared_draws(key):
    memory = jax.random.truncated_normal(jax.random.fold_in(key, 101), -6.0, 6.0, (SRC, D), jnp.float32)
    w_key = jax.random.truncated_normal(jax.random.fold_in(key, 102), -6.0, 6.0, (D, INNER), jnp.float32) * D ** (-0.5)
    query = jax.random.truncated_normal(jax.random.fold_in(key, 103), -6.0, 6.0, (TGT, INNER), jnp.float32)
    return (memory, w_key, query)


def draw_memory(key, part):
    return shared_draws(key)[0].astype(jnp.bfloat16)


def draw_w_key(key, part):
    return shared_draws(key)[1].astype(jnp.bfloat16)


def draw_query(key, part):
    return shared_draws(key)[2].astype(jnp.bfloat16)


def steps_of(own_key, extent, split, least, high):
    loudness, own = 1.0, jax.random.fold_in(own_key, 6)
    for axis_at, blocks in split:
        draws = jnp.exp(jax.random.uniform(jax.random.fold_in(own, axis_at), (blocks,), jnp.float32, least / len(split), high / len(split)))
        loudness = loudness * jnp.repeat(draws, extent[axis_at] // blocks).reshape([-1 if axis == axis_at else 1 for axis in range(len(extent))])
    return loudness


def centred(rng, dims, deviation, reach, pieces=(), held_as=jnp.bfloat16):
    loudness = steps_of(rng, dims, pieces, -0.22, 0.18) if pieces else 1.0
    entries = jax.random.normal(rng, dims, jnp.float32) * deviation * loudness
    return jnp.minimum(jnp.maximum(entries, -reach), reach).astype(held_as)


def setup_inputs(seed: int = 0) -> dict:
    seeds = jax.random.split(jax.random.key(seed), 6)
    memory = draw_memory(jax.random.fold_in(seeds[5], 71), 0)
    query = draw_query(jax.random.fold_in(seeds[5], 71), 0)
    out_grad = centred(seeds[2], (TGT, INNER), 16.0, 96.0, ((0, 32), (1, 8)))
    w_key = draw_w_key(jax.random.fold_in(seeds[5], 71), 0)
    w_value = centred(seeds[4], (D, INNER), D ** -0.5, 0.09375, ((1, 8),))
    return dict(memory=memory, query=query, out_grad=out_grad, w_key=w_key, w_value=w_value)


def head_grads(query_head, grad_head, key_head, value_head):
    factor = 1.0 / math.sqrt(HD)
    block_rows = math.gcd(TGT, 2048)
    query_blocks = query_head.reshape(TGT // block_rows, block_rows, HD)
    grad_blocks = grad_head.reshape(TGT // block_rows, block_rows, HD)

    def advance(totals, pair):
        query_block, grad_block = pair
        scores = jnp.dot(query_block, key_head.T, preferred_element_type=jnp.float32) * factor
        weights = jax.nn.softmax(scores, axis=-1)
        weights_low = weights.astype(jnp.bfloat16)
        attended = jnp.dot(weights_low, value_head, preferred_element_type=jnp.float32)
        row_delta = lax.optimization_barrier(jnp.sum(grad_block.astype(jnp.float32) * attended, axis=-1, keepdims=True))
        prob_grad = jnp.dot(grad_block, value_head.T, preferred_element_type=jnp.float32)
        score_grad = (weights * (prob_grad - row_delta) * factor).astype(jnp.bfloat16)
        query_grad = jnp.dot(score_grad, key_head, preferred_element_type=jnp.float32).astype(jnp.bfloat16)
        key_total = totals[0] + jnp.dot(score_grad.T, query_block, preferred_element_type=jnp.float32)
        value_total = totals[1] + jnp.dot(weights_low.T, grad_block, preferred_element_type=jnp.float32)
        return ((key_total, value_total), query_grad)
    start = (jnp.zeros((SRC, HD), jnp.float32), jnp.zeros((SRC, HD), jnp.float32))
    totals, query_grad = lax.scan(advance, start, (query_blocks, grad_blocks))
    return (query_grad.reshape(TGT, HD), totals[0], totals[1])

def reference(memory, query, out_grad, w_key, w_value):
    key_rows = jnp.dot(memory, w_key, preferred_element_type=jnp.float32).astype(jnp.bfloat16)
    value_rows = jnp.dot(memory, w_value, preferred_element_type=jnp.float32).astype(jnp.bfloat16)
    query_heads = query.reshape(TGT, HEADS, HD).transpose(1, 0, 2)
    grad_heads = out_grad.reshape(TGT, HEADS, HD).transpose(1, 0, 2)
    key_heads = key_rows.reshape(SRC, HEADS, HD).transpose(1, 0, 2)
    value_heads = value_rows.reshape(SRC, HEADS, HD).transpose(1, 0, 2)
    query_grad, key_grad, value_grad = lax.map(lambda four: head_grads(*four), (query_heads, grad_heads, key_heads, value_heads))
    d_query = query_grad.transpose(1, 0, 2).reshape(TGT, INNER)
    key_low = key_grad.transpose(1, 0, 2).reshape(SRC, INNER).astype(jnp.bfloat16)
    value_low = value_grad.transpose(1, 0, 2).reshape(SRC, INNER).astype(jnp.bfloat16)
    total = jnp.dot(key_low, w_key.T, preferred_element_type=jnp.float32) + jnp.dot(value_low, w_value.T, preferred_element_type=jnp.float32)
    return (d_query, total.astype(jnp.bfloat16))
```

```python
import math

import jax
import jax.numpy as jnp
from jax import lax
from jax.experimental import pallas as pl
from jax.experimental.pallas import tpu as pltpu
from jax.sharding import PartitionSpec as P

HD = 64
BF = jnp.bfloat16
F32 = jnp.float32
MESH = pl.DeviceIdType.MESH
EXP2_SCALE = math.log2(math.e) / math.sqrt(HD)
FACTOR = 1.0 / math.sqrt(HD)


def mm(a, b):
    return jnp.dot(a, b, preferred_element_type=F32)


def roll64(a):
    return pltpu.roll(a, 64, 1)


def kernel(
    mem_hbm, q_hbm, g_hbm, wk_hbm, wv_hbm, dq_out, dm_out,
    wk, wv, wp, qin, gin, mem, kvl, kv, kvt, qgs, qg, qz, qt, gt, gz,
    sc, ex, ds, mx, ls, att, dlt, dqt, sb_s, sb_r, rs_s, rs_r, zb_s, zb, dq_s, dq_r,
    pm, em, fs, fo,
    in_sem, a_ss, a_rs, b_ss, b_rs, q_ss, q_rs, kz_ss, ky_ss, kf_ss, kb_ss, k_rs,
    sb_ss, sb_rs, r_ss, r_rs, z_ss, z_rs, d_ss, d_rs, e_ss, e_rs, f_ss, f_rs,
):
    s = lax.axis_index("seq")
    c = lax.axis_index("col")
    y, zh, j = s // 8, (s // 2) % 4, s % 2
    x, zl = c // 2, c % 2

    def at_seq(yy, zz, jj):
        return ((yy * 4 + zz) * 2 + jj, c)

    def send(src, dst, ss, rs, to):
        d = pltpu.make_async_remote_copy(
            src_ref=src, dst_ref=dst, send_sem=ss, recv_sem=rs,
            device_id=to, device_id_type=MESH,
        )
        d.start()
        return d

    def arrived(ref, rs):
        pltpu.make_async_remote_copy(
            src_ref=ref, dst_ref=ref, send_sem=rs, recv_sem=rs,
            device_id=(s, c), device_id_type=MESH,
        ).wait_recv()

    def sent(ref, ss):
        pltpu.make_async_remote_copy(
            src_ref=ref, dst_ref=ref, send_sem=ss, recv_sem=ss,
            device_id=(s, c), device_id_type=MESH,
        ).wait_send()

    barrier = pltpu.get_barrier_semaphore()

    @pl.loop(1, 32)
    def _(k):
        pl.semaphore_signal(barrier, inc=1, device_id=((s + k) % 32, c), device_id_type=MESH)

    @pl.loop(1, 8)
    def _(k):
        pl.semaphore_signal(barrier, inc=1, device_id=(s, (c + k) % 8), device_id_type=MESH)

    loads = [
        pltpu.make_async_copy(q_hbm, qin, in_sem.at[0]),
        pltpu.make_async_copy(g_hbm, gin, in_sem.at[1]),
        pltpu.make_async_copy(wk_hbm, wk, in_sem.at[2]),
        pltpu.make_async_copy(wv_hbm, wv, in_sem.at[3]),
        pltpu.make_async_copy(
            mem_hbm.at[s], mem.at[c, :, pl.ds(pl.multiple_of(s * 128, 128), 128)], in_sem.at[4]
        ),
    ]
    for ld in loads:
        ld.start()

    pl.semaphore_wait(barrier, 38)

    my_cols = pl.ds(pl.multiple_of(s * 128, 128), 128)

    @pl.loop(1, 32)
    def _(k):
        o = (s + k) % 32
        send(mem_hbm.at[o], mem.at[c, :, my_cols], a_ss.at[o], a_rs.at[s], (o, c))

    loads[0].wait()
    loads[1].wait()
    low = lax.broadcasted_iota(jnp.int32, (256, 128), 1) < HD
    for t in range(2):
        qtile = qin[:, t * 128 : (t + 1) * 128].astype(F32)
        gtile = gin[:, t * 128 : (t + 1) * 128].astype(F32)
        qgs[2 * t] = jnp.where(low, qtile, roll64(gtile)).astype(BF)
        qgs[2 * t + 1] = jnp.where(low, roll64(qtile), gtile).astype(BF)
    for k in (1, 3, 2):
        h = (zh + k) % 4
        send(qgs.at[h], qg.at[zh], q_ss.at[k], q_rs.at[zh], at_seq(y, h, j))
    qg[zh] = qgs[zh]

    loads[2].wait()
    loads[3].wait()
    low_w = lax.broadcasted_iota(jnp.int32, (256, 128), 1) < HD

    @pl.loop(0, 16)
    def _(i):
        rows = pl.ds(pl.multiple_of(i * 256, 256), 256)
        for t in range(2):
            kt = wk[rows, t * 128 : (t + 1) * 128].astype(F32)
            vt = wv[rows, t * 128 : (t + 1) * 128].astype(F32)
            wp[rows, 2 * t * 128 : (2 * t + 1) * 128] = jnp.where(low_w, kt, roll64(vt)).astype(BF)
            wp[rows, (2 * t + 1) * 128 : (2 * t + 2) * 128] = jnp.where(
                low_w, roll64(kt), vt
            ).astype(BF)

    loads[4].wait()

    @pl.loop(1, 32)
    def _(k):
        o = (s + k) % 32
        arrived(mem.at[c, :, pl.ds(pl.multiple_of(o * 128, 128), 128)], a_rs.at[o])

    def col(xx, zz):
        return xx * 2 + zz

    x1, x2, x3, ol = (x + 1) % 4, (x + 2) % 4, (x + 3) % 4, 1 - zl
    for n, to in enumerate((col(x, ol), col(x1, zl), col(x3, zl), col(x2, zl))):
        send(mem.at[c], mem.at[c], b_ss.at[n], b_rs.at[c], (s, to))
    p = col(x, ol)
    arrived(mem.at[p], b_rs.at[p])
    send(mem.at[p], mem.at[p], b_ss.at[4], b_rs.at[p], (s, col(x1, zl)))
    send(mem.at[p], mem.at[p], b_ss.at[5], b_rs.at[p], (s, col(x3, zl)))
    p2 = col(x2, zl)
    arrived(mem.at[p2], b_rs.at[p2])
    send(mem.at[p2], mem.at[p2], b_ss.at[6], b_rs.at[p2], (s, col(x, ol)))
    for p in (col(x1, zl), col(x3, zl), col(x1, ol), col(x3, ol), col(x2, ol)):
        arrived(mem.at[p], b_rs.at[p])

    rows_all = mem[...].reshape(128, 4096)
    kv_new = mm(rows_all, wp[...]).astype(BF)
    for h in range(4):
        kvl[h] = kv_new[:, h * 128 : (h + 1) * 128]

    def slot(jj, yy, zz):
        return kv.at[jj * 4 + yy, pl.ds(pl.multiple_of(zz * 128, 128), 128)]

    def slot_sem(jj, yy, zz):
        return k_rs.at[(jj * 4 + yy) * 4 + zz]

    for k in (1, 3, 2):
        h = (zh + k) % 4
        send(kvl.at[h], slot(j, y, zh), kz_ss.at[k], slot_sem(j, y, zh), at_seq(y, h, j))
    slot(j, y, zh)[...] = kvl[zh]
    y1, y2, y3, oj = (y + 1) % 4, (y + 2) % 4, (y + 3) % 4, 1 - j

    def share(yy, zz, sem, to):
        send(slot(j, yy, zz), slot(j, yy, zz), sem, slot_sem(j, yy, zz), to)

    for k in (0, 1, 3, 2):
        zz = (zh + k) % 4
        if k:
            arrived(slot(j, y, zz), slot_sem(j, y, zz))
        share(y, zz, ky_ss.at[0, k], at_seq(y1, zh, j))
        share(y, zz, ky_ss.at[1, k], at_seq(y3, zh, j))
        share(y, zz, kb_ss.at[0, k], at_seq(y, zh, oj))

    low_q = lax.broadcasted_iota(jnp.int32, (256, 128), 1) < HD
    low_t = lax.broadcasted_iota(jnp.int32, (128, 256), 0) < HD
    for k in (0, 1, 3, 2):
        b = (zh + k) % 4
        if k:
            arrived(qg.at[b], q_rs.at[b])
    for b in range(4):
        both = qg[b].astype(F32)
        qz[b] = jnp.where(low_q, both, 0.0).astype(BF)
        turned = both.T
        qt[:, b * 256 : (b + 1) * 256] = jnp.where(low_t, turned, 0.0).astype(BF)
        gt[:, b * 256 : (b + 1) * 256] = jnp.where(low_t, 0.0, turned)
    mx[...] = jnp.full((8, 1024), -jnp.inf, F32)

    def scores(ch):
        for r in range(2):
            part = kv[ch, r * 256 : (r + 1) * 256, :]
            kvt[ch, :, r * 256 : (r + 1) * 256] = part.astype(F32).T.astype(BF)
            for b in range(4):
                cols = slice(b * 256, (b + 1) * 256)
                v = mm(part, qt[:, cols])
                sc[ch, r * 256 : (r + 1) * 256, cols] = v
                mx[:, cols] = jnp.maximum(mx[:, cols], v.reshape(32, 8, 256).max(axis=0))

    scores(j * 4 + y)
    for zz in range(4):
        arrived(slot(j, y3, zz), slot_sem(j, y3, zz))
        share(y3, zz, kb_ss.at[1, zz], at_seq(y, zh, oj))
        if zz < 2:
            share(y3, zz, kf_ss.at[zz], at_seq(y1, zh, j))
        arrived(slot(j, y1, zz), slot_sem(j, y1, zz))
        share(y1, zz, kb_ss.at[2, zz], at_seq(y, zh, oj))
        if zz >= 2:
            share(y1, zz, kf_ss.at[zz], at_seq(y3, zh, j))
    for zz in range(4):
        arrived(slot(j, y2, zz), slot_sem(j, y2, zz))
        share(y2, zz, kb_ss.at[3, zz], at_seq(y, zh, oj))

    @pl.loop(1, 4)
    def _(k):
        scores(j * 4 + (y + k) % 4)

    @pl.loop(0, 16)
    def _(i):
        zz, yy = i % 4, i // 4
        arrived(slot(oj, yy, zz), slot_sem(oj, yy, zz))

    @pl.loop(0, 4)
    def _(k):
        scores(oj * 4 + k)

    mx[...] = jnp.broadcast_to(jnp.max(mx[...], axis=0, keepdims=True), (8, 1024))
    ls[...] = jnp.zeros((8, 1024), F32)
    att[...] = jnp.zeros((128, 1024), F32)

    @pl.loop(0, 8)
    def _(ch):
        for b in range(4):
            cols = slice(b * 256, (b + 1) * 256)
            top = mx[0:1, cols]
            total = jnp.zeros((8, 256), F32)
            for r in range(2):
                rows = slice(r * 256, (r + 1) * 256)
                e = jnp.exp2((sc[ch, rows, cols] - top) * EXP2_SCALE)
                total = total + e.reshape(32, 8, 256).sum(axis=0)
                ex[ch, rows, cols] = e.astype(BF)
            ls[:, cols] += total
            att[:, cols] += mm(kvt[ch], ex[ch, :, cols])

    for b in range(4):
        cols = slice(b * 256, (b + 1) * 256)
        inv = 1.0 / jnp.sum(ls[:, cols], axis=0, keepdims=True)
        scaled = (gt[:, cols] * inv).astype(BF)
        wide = scaled.astype(F32)
        gt[:, cols] = wide
        gz[b] = wide.T.astype(BF)
        dlt[:, cols] = jnp.broadcast_to(
            jnp.sum(wide * (att[:, cols] * inv), axis=0, keepdims=True), (8, 256)
        )
        qt[:, cols] = scaled
    dqt[...] = jnp.zeros((128, 1024), F32)
    low_o = lax.broadcasted_iota(jnp.int32, (512, 128), 1) < HD

    def grads(ch):
        for b in range(4):
            cols = slice(b * 256, (b + 1) * 256)
            delta = dlt[0:1, cols]
            for r in range(2):
                rows = slice(r * 256, (r + 1) * 256)
                pg = mm(kv[ch, rows, :], qt[:, cols])
                ds[rows, cols] = (ex[ch, rows, cols].astype(F32) * (pg - delta)).astype(BF)
            dqt[:, cols] += mm(kvt[ch], ds[:, cols])
        qall = qz[...].reshape(1024, 128)
        gall = gz[...].reshape(1024, 128)
        dk = mm(ds[...], qall)
        dv = mm(ex[ch], gall)
        return jnp.where(low_o, dk * FACTOR, dv)

    @pl.loop(0, 4)
    def _(k):
        yy = (y + 2 + k) % 4
        sb_s[k] = grads(oj * 4 + yy).astype(BF)
        send(sb_s.at[k], sb_r.at[k], sb_ss.at[k], sb_rs.at[k], at_seq(y, zh, oj))

    @pl.loop(0, 3)
    def _(k):
        yy = (y + 2 + k + k // 2) % 4
        mine = grads(j * 4 + yy)
        at = k + k // 2
        arrived(sb_r.at[at], sb_rs.at[at])
        rs_s[k] = (mine + sb_r[at].astype(F32)).astype(BF)
        send(rs_s.at[k], rs_r.at[k], r_ss.at[k], r_rs.at[k], at_seq(yy, zh, j))

    total = grads(j * 4 + y)
    arrived(sb_r.at[2], sb_rs.at[2])
    total = total + sb_r[2].astype(F32)
    for k in range(3):
        arrived(rs_r.at[k], r_rs.at[k])
        total = total + rs_r[k].astype(F32)
    zb_s[...] = total.astype(BF).reshape(4, 128, 128)
    head_cols = pl.ds(pl.multiple_of(zh * 128, 128), 128)
    for k in (1, 3, 2):
        zz = (zh + k) % 4
        send(zb_s.at[zz], zb.at[:, head_cols], z_ss.at[k], z_rs.at[zh], at_seq(y, zz, j))
    zb[:, head_cols] = zb_s[zh]

    low_d = lax.broadcasted_iota(jnp.int32, (128, 128), 1) < HD
    for b in range(4):
        back = (dqt[:, b * 256 : (b + 1) * 256] * FACTOR).T
        dq_s[b] = jnp.where(low_d, back[:128], roll64(back[128:])).astype(BF)
    for k in (1, 3, 2):
        zz = (zh + k) % 4
        send(dq_s.at[zz], dq_r.at[zh], d_ss.at[k], d_rs.at[zh], at_seq(y, zz, j))
    dq_r[zh] = dq_s[zh]

    for k in (1, 3, 2):
        zz = (zh + k) % 4
        arrived(zb.at[:, pl.ds(pl.multiple_of(zz * 128, 128), 128)], z_rs.at[zz])
    lhs = zb[...]
    for n in range(8):
        part = lax.dot_general(
            lhs, wp[n * 512 : (n + 1) * 512, :], (((1,), (1,)), ((), ())),
            preferred_element_type=F32,
        ).astype(BF)
        pm[:, :, n * 512 : (n + 1) * 512] = part.reshape(8, 16, 512)
    for k in (4, 1, 7, 2, 6, 3, 5):
        o = (c + k) % 8
        send(pm.at[o], em.at[c], e_ss.at[k], e_rs.at[c], (s, o))

    for k in (1, 3, 2):
        zz = (zh + k) % 4
        arrived(dq_r.at[zz], d_rs.at[zz])
    for t in range(2):
        a = dq_r[2 * t].astype(F32)
        b = dq_r[2 * t + 1].astype(F32)
        tile = slice(t * 128, (t + 1) * 128)
        dq_out[0:128, tile] = jnp.where(low_d, a, roll64(b)).astype(BF)
        dq_out[128:256, tile] = jnp.where(low_d, roll64(a), b).astype(BF)

    em[c] = pm[c]
    for k in range(1, 8):
        o = (c + k) % 8
        arrived(em.at[o], e_rs.at[o])
    acc = em[0].astype(F32)
    for k in range(1, 8):
        acc = acc + em[k].astype(F32)
    fs[...] = acc.astype(BF)

    @pl.loop(1, 32)
    def _(k):
        o = (s + k) % 32
        send(
            fs.at[:, pl.ds(pl.multiple_of(o * 128, 128), 128)], fo.at[s],
            f_ss.at[o], f_rs.at[s], (o, c),
        )

    fo[s] = fs[:, my_cols]

    @pl.loop(1, 32)
    def _(k):
        o = (s + k) % 32
        arrived(fo.at[o], f_rs.at[o])

    dm_out[...] = fo[...]

    @pl.loop(1, 32)
    def _(k):
        o = (s + k) % 32
        sent(fo.at[o], a_ss.at[o])
        sent(fo.at[o], f_ss.at[o])

    for n in range(7):
        sent(mem.at[0], b_ss.at[n])
        sent(pm.at[0], e_ss.at[n + 1])
    for k in range(1, 4):
        sent(qgs.at[0], q_ss.at[k])
        sent(kvl.at[0], kz_ss.at[k])
        sent(zb_s.at[0], z_ss.at[k])
        sent(dq_s.at[0], d_ss.at[k])
        sent(rs_s.at[0], r_ss.at[k - 1])
    for k in range(4):
        sent(kvl.at[0], ky_ss.at[0, k])
        sent(kvl.at[0], ky_ss.at[1, k])
        sent(kvl.at[0], kf_ss.at[k])
        sent(sb_s.at[0], sb_ss.at[k])
        for n in range(4):
            sent(kvl.at[0], kb_ss.at[n, k])


def local(memory, query, out_grad, w_key, w_value):
    dma = pltpu.SemaphoreType.DMA
    v = pltpu.VMEM
    dq, dm = pl.pallas_call(
        kernel,
        out_shape=(
            jax.ShapeDtypeStruct((256, 256), BF),
            jax.ShapeDtypeStruct((32, 16, 128), BF),
        ),
        in_specs=[pl.BlockSpec(memory_space=pl.ANY)] * 5,
        out_specs=(pl.BlockSpec(memory_space=pltpu.VMEM),) * 2,
        scratch_shapes=[
            v((4096, 256), BF), v((4096, 256), BF), v((4096, 512), BF),
            v((256, 256), BF), v((256, 256), BF),
            v((8, 16, 4096), BF), v((4, 128, 128), BF),
            v((8, 512, 128), BF), v((8, 128, 512), BF),
            v((4, 256, 128), BF), v((4, 256, 128), BF), v((4, 256, 128), BF),
            v((128, 1024), BF), v((128, 1024), F32), v((4, 256, 128), BF),
            v((8, 512, 1024), F32), v((8, 512, 1024), BF), v((512, 1024), BF),
            v((8, 1024), F32), v((8, 1024), F32), v((128, 1024), F32), v((8, 1024), F32),
            v((128, 1024), F32),
            v((4, 512, 128), BF), v((4, 512, 128), BF),
            v((3, 512, 128), BF), v((3, 512, 128), BF),
            v((4, 128, 128), BF), v((128, 512), BF),
            v((4, 128, 128), BF), v((4, 128, 128), BF),
            v((8, 16, 4096), BF), v((8, 16, 4096), BF),
            v((16, 4096), BF), v((32, 16, 128), BF),
            dma((5,)), dma((32,)), dma((32,)), dma((7,)), dma((8,)),
            dma((4,)), dma((4,)), dma((4,)), dma((2, 4)), dma((4,)), dma((4, 4)), dma((32,)),
            dma((4,)), dma((4,)), dma((3,)), dma((3,)), dma((4,)), dma((4,)),
            dma((4,)), dma((4,)), dma((8,)), dma((8,)), dma((32,)), dma((32,)),
        ],
        compiler_params=pltpu.CompilerParams(
            collective_id=0, has_side_effects=True, vmem_limit_bytes=60 * 1024 * 1024
        ),
    )(memory.reshape(32, 16, 128), query, out_grad, w_key, w_value)
    return dq, dm.reshape(512, 128)


def solution(mesh):
    return jax.shard_map(
        local,
        mesh=mesh,
        in_specs=(
            P("col", "seq"),
            P("seq", "col"),
            P("seq", "col"),
            P(None, "col"),
            P(None, "col"),
        ),
        out_specs=(P("seq", "col"), P("col", "seq")),
        check_vma=False,
    )
```

```python
import math

import jax
import jax.numpy as jnp
from jax import lax
from jax.experimental import pallas as pl
from jax.experimental.pallas import tpu as pltpu
from jax.sharding import PartitionSpec as P

HD = 64
BF = jnp.bfloat16
F32 = jnp.float32
MESH = pl.DeviceIdType.MESH
EXP2_SCALE = math.log2(math.e) / math.sqrt(HD)
FACTOR = 1.0 / math.sqrt(HD)


def mm(a, b):
    return jnp.dot(a, b, preferred_element_type=F32)


def mm_t(a, b):
    return lax.dot_general(a, b, (((1,), (1,)), ((), ())), preferred_element_type=F32)


def roll64(a):
    return pltpu.roll(a, 64, 1)


def kernel(
    mem_hbm, q_hbm, g_hbm, wk_hbm, wv_hbm, dq_out, dm_out,
    wk, wv, wp, qin, gin, mem, kvl, kv, kvt, q_s, q_r, g_s, g_r, qt, gt, gs,
    sc, ex, ds, mx, tops, ls, att, dqt, gk, sb_s, sb_r, rs_s, rs_r, tot, zb_s, zb, dq_s, dq_r,
    pm, e1_r, e2_s, e2_r, fs, fo,
    in_sem, ss, a_rs, b_rs, k_rs, sb_rs, r_rs, d_rs, e_rs,
):
    s = lax.axis_index("seq")
    c = lax.axis_index("col")
    y, zh, j = s // 8, (s // 2) % 4, s % 2
    x, zl = c // 2, c % 2

    def at_seq(yy, zz, jj):
        return ((yy * 4 + zz) * 2 + jj, c)

    def send(src, dst, ss, rs, to):
        d = pltpu.make_async_remote_copy(
            src_ref=src, dst_ref=dst, send_sem=ss, recv_sem=rs,
            device_id=to, device_id_type=MESH,
        )
        d.start()
        return d

    def arrived(ref, rs):
        pltpu.make_async_remote_copy(
            src_ref=ref, dst_ref=ref, send_sem=rs, recv_sem=rs,
            device_id=(s, c), device_id_type=MESH,
        ).wait_recv()

    def sent(ref, ss):
        pltpu.make_async_remote_copy(
            src_ref=ref, dst_ref=ref, send_sem=ss, recv_sem=ss,
            device_id=(s, c), device_id_type=MESH,
        ).wait_send()

    barrier = pltpu.get_barrier_semaphore()

    @pl.loop(1, 32)
    def _(k):
        pl.semaphore_signal(barrier, inc=1, device_id=((s + k) % 32, c), device_id_type=MESH)

    @pl.loop(1, 8)
    def _(k):
        pl.semaphore_signal(barrier, inc=1, device_id=(s, (c + k) % 8), device_id_type=MESH)

    loads = [
        pltpu.make_async_copy(q_hbm, qin, in_sem.at[0]),
        pltpu.make_async_copy(g_hbm, gin, in_sem.at[1]),
        pltpu.make_async_copy(wk_hbm, wk, in_sem.at[2]),
        pltpu.make_async_copy(wv_hbm, wv, in_sem.at[3]),
        pltpu.make_async_copy(
            mem_hbm.at[s],
            mem.at[zh, c, :, pl.ds(pl.multiple_of((y * 2 + j) * 128, 128), 128)],
            in_sem.at[4],
        ),
    ]
    for ld in loads:
        ld.start()

    pl.semaphore_wait(barrier, 38)

    my_cols = pl.ds(pl.multiple_of((y * 2 + j) * 128, 128), 128)
    near = (0, 1, 3, 2)

    def feature_group(dz, act):
        @pl.loop(0 if dz else 1, 8)
        def _(m):
            oy, oc = (y + m // 2) % 4, (j + m) % 2
            cols = pl.ds(pl.multiple_of((oy * 2 + oc) * 128, 128), 128)
            act((oy * 4 + (zh + dz) % 4) * 2 + oc, cols)

    back = (0, 2, 1, 3)
    for n, dz in enumerate(near):
        feature_group(
            dz,
            lambda o, cols: send(
                mem_hbm.at[o], mem.at[zh, c, :, my_cols], ss.at[0], a_rs.at[back[n]], (o, c)
            ),
        )

    low = lax.broadcasted_iota(jnp.int32, (128, 128), 1) < HD

    def halves(top, bottom):
        return (
            jnp.where(low, top, roll64(bottom)).astype(BF),
            jnp.where(low, roll64(top), bottom).astype(BF),
        )

    def pack_heads(rows, out):
        for t in range(2):
            tile = slice(t * 128, (t + 1) * 128)
            out[2 * t], out[2 * t + 1] = halves(
                rows[0:128, tile].astype(F32), rows[128:256, tile].astype(F32)
            )

    def deal(out, into, which):
        for k in (1, 3, 2):
            h = (zh + k) % 4
            send(out.at[h], into.at[zh], ss.at[which], d_rs.at[which], at_seq(y, h, j))
        into[zh] = out[zh]

    def dealt(into, which):
        arrived(into.at[pl.ds(0, 3)], d_rs.at[which])

    loads[0].wait()
    loads[1].wait()
    pack_heads(qin, q_s)
    pack_heads(gin, g_s)

    loads[2].wait()
    loads[3].wait()
    low_w = lax.broadcasted_iota(jnp.int32, (256, 128), 1) < HD

    @pl.loop(0, 16)
    def _(i):
        rows = pl.ds(pl.multiple_of(i * 256, 256), 256)
        sub = pl.ds(pl.multiple_of(i // 4 * 256, 256), 256)
        for t in range(2):
            kt = wk[rows, t * 128 : (t + 1) * 128].astype(F32)
            vt = wv[rows, t * 128 : (t + 1) * 128].astype(F32)
            wp[i % 4, sub, 2 * t * 128 : (2 * t + 1) * 128] = jnp.where(low_w, kt, roll64(vt)).astype(BF)
            wp[i % 4, sub, (2 * t + 1) * 128 : (2 * t + 2) * 128] = jnp.where(
                low_w, roll64(kt), vt
            ).astype(BF)

    loads[4].wait()

    def col(xx, zz):
        return xx * 2 + zz

    x1, x2, x3, ol = (x + 1) % 4, (x + 2) % 4, (x + 3) % 4, 1 - zl

    def quarter(n):
        return (zh + near[n]) % 4

    def pass_on(p, n, which, to):
        here = mem.at[quarter(n), p]
        send(here, here, ss.at[4], b_rs.at[n, which], (s, to))

    def own_rows(n):
        if n:
            arrived(mem.at[quarter(n), c], a_rs.at[n])
        else:
            arrived(fo.at[pl.ds(0, 7)], a_rs.at[n])
        pass_on(c, n, 2, col(x1, zl))
        pass_on(c, n, 2, col(x3, zl))
        pass_on(c, n, 0, col(x, ol))
        pass_on(c, n, 1, col(x2, zl))

    def relay_near(n):
        arrived(mem.at[quarter(n), 0], b_rs.at[n, 0])
        pass_on(col(x, ol), n, 2, col(x1, zl))
        pass_on(col(x, ol), n, 2, col(x3, zl))

    def relay_far(n):
        arrived(mem.at[quarter(n), 0], b_rs.at[n, 1])
        pass_on(col(x2, zl), n, 2, col(x, ol))

    own_rows(0)
    own_rows(1)
    relay_near(0)
    own_rows(2)
    relay_near(1)
    own_rows(3)
    deal(q_s, q_r, 1)
    relay_far(0)
    relay_near(2)
    relay_far(1)
    relay_near(3)
    relay_far(2)
    relay_far(3)

    kv_new = jnp.zeros((128, 512), F32)
    for n in range(4):
        arrived(mem.at[quarter(n), pl.ds(0, 5)], b_rs.at[n, 2])
        kv_new = kv_new + mm(mem[quarter(n)].reshape(128, 1024), wp[quarter(n)])
    kv_new = kv_new.astype(BF)
    for h in range(4):
        kvl[h] = kv_new[:, h * 128 : (h + 1) * 128]

    def slot(jj, yy, zz):
        return kv.at[jj * 4 + yy, pl.ds(pl.multiple_of(zz * 128, 128), 128)]

    for k in (1, 3, 2):
        h = (zh + k) % 4
        send(kvl.at[h], slot(j, y, zh), ss.at[12], k_rs.at[4 - k], at_seq(y, h, j))
    slot(j, y, zh)[...] = kvl[zh]
    deal(g_s, g_r, 2)
    y1, y2, y3, oj = (y + 1) % 4, (y + 2) % 4, (y + 3) % 4, 1 - j

    def share(yy, zz, sem, to):
        send(slot(j, yy, zz), slot(j, yy, zz), ss.at[5], k_rs.at[sem], to)

    for n, k in enumerate(near):
        zz = (zh + k) % 4
        if k:
            arrived(slot(j, y, zz), k_rs.at[k])
        share(y, zz, 4 + n, at_seq(y1, zh, j))
        share(y, zz, 8 + n, at_seq(y3, zh, j))
        share(y, zz, 13, at_seq(y, zh, oj))

    qt[HD:, :] = jnp.zeros((HD, 1024), BF)
    dealt(q_r, 1)
    for b in range(4):
        turned = q_r[b].astype(F32).T.astype(BF)
        qt[0:HD, b * 256 : b * 256 + 128] = turned[:HD]
        qt[0:HD, b * 256 + 128 : (b + 1) * 256] = turned[HD:]
    mx[...] = jnp.full((8, 1024), -jnp.inf, F32)
    ls[...] = jnp.zeros((8, 1024), F32)
    att[...] = jnp.zeros((HD, 1024), F32)

    def stage(body):
        @pl.loop(0, 1)
        def _(_):
            for b in range(4):
                body(slice(b * 256, (b + 1) * 256))

    def attend(ch):
        def score(cols):
            top = jnp.full((8, 256), -jnp.inf, F32)
            for r in range(2):
                rows = slice(r * 256, (r + 1) * 256)
                v = mm(kv[ch, rows, :], qt[:, cols])
                sc[rows, cols] = v
                top = jnp.maximum(top, v.reshape(32, 8, 256).max(axis=0))
            top = jnp.maximum(mx[0:1, cols], jnp.max(top, axis=0, keepdims=True))
            tops[ch, :, cols] = jnp.broadcast_to(top, (8, 256))

        def weigh(cols):
            top = tops[ch, 0:1, cols]
            shrink = jnp.exp2((mx[0:1, cols] - top) * EXP2_SCALE)
            mx[:, cols] = tops[ch, :, cols]
            total = ls[:, cols] * shrink
            for r in range(2):
                rows = slice(r * 256, (r + 1) * 256)
                e = jnp.exp2((sc[rows, cols] - top) * EXP2_SCALE)
                total = total + e.reshape(32, 8, 256).sum(axis=0)
                ex[ch, rows, cols] = e.astype(BF)
            ls[:, cols] = total
            att[:, cols] = att[:, cols] * shrink + mm(kvt[ch, HD:, :], ex[ch, :, cols])

        for r in range(2):
            rows = slice(r * 256, (r + 1) * 256)
            kvt[ch, :, rows] = kv[ch, rows, :].astype(F32).T.astype(BF)
        stage(score)
        stage(weigh)

    attend(j * 4 + y)
    for n, k in enumerate(near):
        zz = (zh + k) % 4
        arrived(slot(j, y3, zz), k_rs.at[4 + n])
        if n < 2:
            share(y3, zz, 12, at_seq(y1, zh, j))
        share(y3, zz, 16, at_seq(y, zh, oj))
        arrived(slot(j, y1, zz), k_rs.at[8 + n])
        if n >= 2:
            share(y1, zz, 12, at_seq(y3, zh, j))
        share(y1, zz, 14, at_seq(y, zh, oj))

    @pl.loop(0, 7)
    def _(i):
        k = jnp.where(i == 0, 3, jnp.where(i == 1, 1, jnp.where(i == 2, 2, 0)))
        k = jnp.where(i < 3, k, jnp.where(i == 4, 3, jnp.where(i == 5, 1, jnp.where(i == 6, 2, k))))
        yy = (y + k) % 4

        @pl.when(i == 1)
        def _():
            far = kv.at[j * 4 + y2]
            arrived(far, k_rs.at[12])
            send(far, far, ss.at[5], k_rs.at[15], at_seq(y, zh, oj))

        @pl.when(i >= 3)
        def _():
            arrived(kv.at[oj * 4 + yy], k_rs.at[13 + k])

        attend(jnp.where(i < 3, j, oj) * 4 + yy)

    dealt(g_r, 2)
    gs[0:HD, :] = jnp.zeros((HD, 1024), BF)
    for b in range(4):
        cols = slice(b * 256, (b + 1) * 256)
        turned = g_r[b].astype(F32).T
        inv = 1.0 / jnp.sum(ls[:, cols], axis=0, keepdims=True)
        gt[:, b * 256 : b * 256 + 128] = turned[:HD] * inv[:, :128]
        gt[:, b * 256 + 128 : (b + 1) * 256] = turned[HD:] * inv[:, 128:]
        att[:, cols] = att[:, cols] * inv
    dqt[...] = jnp.zeros((HD, 1024), F32)

    def grads(ch):
        def score_grad(cols):
            shrink = jnp.exp2((tops[ch, 0:1, cols] - mx[0:1, cols]) * EXP2_SCALE)
            scaled = (gt[:, cols] * shrink).astype(BF)
            gs[HD:, cols] = scaled
            delta = jnp.sum(scaled.astype(F32) * att[:, cols], axis=0, keepdims=True)
            for r in range(2):
                rows = slice(r * 256, (r + 1) * 256)
                pg = mm(kv[ch, rows, :], gs[:, cols])
                ds[rows, cols] = (ex[ch, rows, cols].astype(F32) * (pg - delta)).astype(BF)

        def query_grad(cols):
            dqt[:, cols] += mm(kvt[ch, 0:HD, :], ds[:, cols])

        stage(score_grad)
        stage(query_grad)
        dk = mm_t(qt[0:HD, :], ds[...]) * FACTOR
        dv = mm_t(gs[HD:, :], ex[ch])
        for zz in range(4):
            gk[zz, 0:HD, :] = dk[:, zz * 128 : (zz + 1) * 128]
            gk[zz, HD:, :] = dv[:, zz * 128 : (zz + 1) * 128]

    at_kz = tuple((zh + k) % 4 for k in (1, 3, 2, 0))

    @pl.loop(0, 8)
    def _(i):
        mine = (i == 2) | (i == 4) | (i == 5) | (i == 7)
        far = jnp.where(i < 4, jnp.where(i == 3, 3, jnp.where(i == 1, 1, 0)), 2)
        k = jnp.where(i == 4, 1, jnp.where(i == 5, 3, far))
        yy = (y + 2 + k) % 4
        grads(jnp.where(mine, j, oj) * 4 + yy)

        @pl.when(jnp.logical_not(mine))
        def _():
            sb_s[k] = gk[...].astype(BF)
            send(sb_s.at[k], sb_r.at[k], ss.at[6], sb_rs.at[k], at_seq(y, zh, oj))

        @pl.when(mine)
        def _():
            arrived(sb_r.at[k], sb_rs.at[k])
            both = gk[...] + sb_r[k].astype(F32)

            @pl.when(k == 2)
            def _():
                tot[...] = both

            @pl.when(k != 2)
            def _():
                at = k - k // 3
                rs_s[at] = both.astype(BF)
                for n, zz in enumerate(at_kz):
                    send(
                        rs_s.at[at, zz], rs_r.at[at, zz], ss.at[11], r_rs.at[n],
                        at_seq(yy, zh, j),
                    )

    for b in range(4):
        pair = [dqt[:, b * 256 + r * 128 : b * 256 + (r + 1) * 128] * FACTOR for r in range(2)]
        dq_s[b] = jnp.concatenate(pair, axis=0).T.astype(BF)

    head_cols = pl.ds(pl.multiple_of(zh * 128, 128), 128)
    for n, zz in enumerate(at_kz):
        acc = tot[zz]
        arrived(rs_r.at[pl.ds(0, 3), 0], r_rs.at[n])
        for k in range(3):
            acc = acc + rs_r[k, zz].astype(F32)
        acc = acc.T
        if n < 3:
            zb_s[zz] = acc.astype(BF)
            send(zb_s.at[zz], zb.at[:, head_cols], ss.at[7], d_rs.at[0], at_seq(y, zz, j))
        else:
            zb[:, head_cols] = acc.astype(BF)

    arrived(zb.at[:, pl.ds(0, 384)], d_rs.at[0])
    lhs = zb[...]
    far_first = (2, 3, 1, 0)

    def partial(n):
        zq = (zh + far_first[n]) % 4
        for r in range(2):
            part = mm_t(lhs, wp[zq, r * 512 : (r + 1) * 512, :]).astype(BF)
            pm[n, :, :, r * 512 : (r + 1) * 512] = part.reshape(8, 16, 512)
        for i, (block, to) in enumerate((
            (col(x2, ol), col(x, ol)),
            (col(x1, ol), col(x1, zl)),
            (col(x3, ol), col(x3, zl)),
            (col(x1, zl), col(x1, zl)),
            (col(x3, zl), col(x3, zl)),
        )):
            send(pm.at[n, block], e1_r.at[n, i], ss.at[8], e_rs.at[n, (i + 1) // 2], (s, to))

    def combine(n):
        arrived(e1_r.at[n, 0], e_rs.at[n, 0])
        e2_s[n, 0] = (e1_r[n, 0].astype(F32) + pm[n, col(x2, zl)].astype(F32)).astype(BF)
        send(e2_s.at[n, 0], e2_r.at[n, 0], ss.at[9], e_rs.at[n, 2], (s, col(x2, zl)))
        arrived(e1_r.at[n, pl.ds(1, 2)], e_rs.at[n, 1])
        e2_s[n, 1] = (
            e1_r[n, 1].astype(F32) + e1_r[n, 2].astype(F32) + pm[n, col(x, ol)].astype(F32)
        ).astype(BF)
        send(e2_s.at[n, 1], e2_r.at[n, 1], ss.at[9], e_rs.at[n, 2], (s, col(x, ol)))

    def finish(n):
        acc = pm[n, c].astype(F32)
        arrived(e1_r.at[n, pl.ds(0, 4)], e_rs.at[n, 2])
        for i in range(2):
            acc = acc + e1_r[n, 3 + i].astype(F32) + e2_r[n, i].astype(F32)
        fs[n] = acc.astype(BF)
        feature_group(
            far_first[n],
            lambda o, cols: send(
                fs.at[n, :, cols], fo.at[s],
                ss.at[10], d_rs.at[4], (o, c),
            ),
        )

    for n in range(4):
        partial(n)
    deal(dq_s, dq_r, 3)
    combine(0)
    combine(1)
    finish(0)
    combine(2)
    finish(1)
    combine(3)

    dealt(dq_r, 3)
    for t in range(2):
        a = dq_r[2 * t].astype(F32)
        b = dq_r[2 * t + 1].astype(F32)
        tile = slice(t * 128, (t + 1) * 128)
        dq_out[0:128, tile], dq_out[128:256, tile] = halves(a, b)

    finish(2)
    finish(3)
    fo[s] = fs[3, :, my_cols]
    arrived(fo.at[pl.ds(0, 31)], d_rs.at[4])

    dm_out[...] = fo[...]

    for n, ref in enumerate((
        fo.at[pl.ds(0, 31)], kvl.at[pl.ds(0, 3)], kvl.at[pl.ds(0, 3)], kvl.at[pl.ds(0, 3)],
        mem.at[:, pl.ds(0, 7)], kv.at[pl.ds(0, 7)], sb_s, kvl.at[pl.ds(0, 3)],
        e1_r, e2_s, fo.at[pl.ds(0, 31)], rs_s, kvl.at[pl.ds(0, 3)],
    )):
        sent(ref, ss.at[n])


def local(memory, query, out_grad, w_key, w_value):
    dma = pltpu.SemaphoreType.DMA
    v = pltpu.VMEM
    dq, dm = pl.pallas_call(
        kernel,
        out_shape=(
            pltpu.VMEM((256, 256), BF),
            pltpu.VMEM((32, 16, 128), BF),
        ),
        in_specs=[pl.BlockSpec(memory_space=pl.ANY)] * 5,
        out_specs=(pl.BlockSpec(memory_space=pltpu.VMEM),) * 2,
        scratch_shapes=[
            v((4096, 256), BF), v((4096, 256), BF), v((4, 1024, 512), BF),
            v((256, 256), BF), v((256, 256), BF),
            v((4, 8, 16, 1024), BF), v((4, 128, 128), BF),
            v((8, 512, 128), BF), v((8, 128, 512), BF),
            v((4, 128, 128), BF), v((4, 128, 128), BF), v((4, 128, 128), BF), v((4, 128, 128), BF),
            v((128, 1024), BF), v((HD, 1024), F32), v((128, 1024), BF),
            v((512, 1024), F32), v((8, 512, 1024), BF), v((512, 1024), BF),
            v((8, 1024), F32), v((8, 8, 1024), F32), v((8, 1024), F32), v((HD, 1024), F32),
            v((HD, 1024), F32), v((4, 128, 128), F32),
            v((4, 4, 128, 128), BF), v((4, 4, 128, 128), BF),
            v((3, 4, 128, 128), BF), v((3, 4, 128, 128), BF), v((4, 128, 128), F32),
            v((4, 128, 128), BF), v((128, 512), BF),
            v((4, 128, 128), BF), v((4, 128, 128), BF),
            v((4, 8, 16, 1024), BF), v((4, 5, 16, 1024), BF),
            v((4, 2, 16, 1024), BF), v((4, 2, 16, 1024), BF),
            v((4, 16, 1024), BF), v((32, 16, 128), BF),
            dma((5,)), dma((13,)), dma((4,)), dma((4, 3)), dma((17,)), dma((4,)), dma((4,)),
            dma((5,)), dma((4, 3)),
        ],
        compiler_params=pltpu.CompilerParams(
            collective_id=0, has_side_effects=True, vmem_limit_bytes=60 * 1024 * 1024
        ),
    )(memory.reshape(32, 16, 128), query, out_grad, w_key, w_value)
    return dq, dm.reshape(512, 128)


def solution(mesh):
    return jax.shard_map(
        local,
        mesh=mesh,
        in_specs=(
            P("col", "seq"),
            P("seq", "col"),
            P("seq", "col"),
            P(None, "col"),
            P(None, "col"),
        ),
        out_specs=(P("seq", "col"), P("col", "seq")),
        check_vma=False,
    )
```

```python
import math

import jax
import jax.numpy as jnp
from jax import lax
from jax.experimental import pallas as pl
from jax.experimental.pallas import tpu as pltpu
from jax.sharding import PartitionSpec as P

HD = 64
BF = jnp.bfloat16
F32 = jnp.float32
MESH = pl.DeviceIdType.MESH
EXP2_SCALE = math.log2(math.e) / math.sqrt(HD)
FACTOR = 1.0 / math.sqrt(HD)


def mm(a, b):
    return jnp.dot(a, b, preferred_element_type=F32)


def mm_t(a, b):
    return lax.dot_general(a, b, (((1,), (1,)), ((), ())), preferred_element_type=F32)


def roll64(a):
    return pltpu.roll(a, 64, 1)


def kernel(
    mem_hbm, q_hbm, g_hbm, wk_hbm, wv_hbm, dq_out, dm_out, held,
    wk, wv, wp, qin, gin, mem, kvl, kv, kvt, q_s, q_r, g_s, g_r, qt, gt, gs,
    sc, ex, ds, mx, tops, shr, ls, att, dqt, gk, sb_s, sb_r, rs_s, rs_r, tot, zb_s, hb, pa, dq_s, dq_r,
    pm, e1_r, e2_s, e2_r, fs, fo,
    in_sem, ss, a_rs, b_rs, k_rs, sb_rs, r_rs, d_rs, e_rs,
):
    s = lax.axis_index("seq")
    c = lax.axis_index("col")
    y, zh, j = s // 8, (s // 2) % 4, s % 2
    x, zl = c // 2, c % 2

    def at_seq(yy, zz, jj):
        return ((yy * 4 + zz) * 2 + jj, c)

    def send(src, dst, ss, rs, to):
        d = pltpu.make_async_remote_copy(
            src_ref=src, dst_ref=dst, send_sem=ss, recv_sem=rs,
            device_id=to, device_id_type=MESH,
        )
        d.start()
        return d

    def arrived(ref, rs):
        pltpu.make_async_remote_copy(
            src_ref=ref, dst_ref=ref, send_sem=rs, recv_sem=rs,
            device_id=(s, c), device_id_type=MESH,
        ).wait_recv()

    def sent(ref, ss):
        pltpu.make_async_remote_copy(
            src_ref=ref, dst_ref=ref, send_sem=ss, recv_sem=ss,
            device_id=(s, c), device_id_type=MESH,
        ).wait_send()

    barrier = pltpu.get_barrier_semaphore()

    @pl.loop(1, 32)
    def _(k):
        pl.semaphore_signal(barrier, inc=1, device_id=((s + k) % 32, c), device_id_type=MESH)

    @pl.loop(1, 8)
    def _(k):
        pl.semaphore_signal(barrier, inc=1, device_id=(s, (c + k) % 8), device_id_type=MESH)

    loads = [
        pltpu.make_async_copy(mem_hbm, held, in_sem.at[5]),
        pltpu.make_async_copy(
            mem_hbm.at[s],
            mem.at[zh, c, :, pl.ds(pl.multiple_of((y * 2 + j) * 128, 128), 128)],
            in_sem.at[4],
        ),
        pltpu.make_async_copy(q_hbm, qin, in_sem.at[0]),
        pltpu.make_async_copy(g_hbm, gin, in_sem.at[1]),
        pltpu.make_async_copy(wk_hbm, wk, in_sem.at[2]),
        pltpu.make_async_copy(wv_hbm, wv, in_sem.at[3]),
    ]
    for ld in loads:
        ld.start()

    loads[0].wait()
    pl.semaphore_wait(barrier, 38)

    my_cols = pl.ds(pl.multiple_of((y * 2 + j) * 128, 128), 128)
    near = (0, 1, 3, 2)

    def far_y(m):
        at = m // 2
        return jnp.where(at == 0, 2, jnp.where(at == 1, 1, jnp.where(at == 2, 3, 0)))

    def feature_group(dz, act):
        @pl.loop(0, 8 if dz else 7)
        def _(m):
            oy, oc = (y + far_y(m)) % 4, (j + 1 + m) % 2
            cols = pl.ds(pl.multiple_of((oy * 2 + oc) * 128, 128), 128)
            act((oy * 4 + (zh + dz) % 4) * 2 + oc, cols)

    back = (0, 2, 1, 3)
    for n in range(4):
        feature_group(
            near[n],
            lambda o, cols: send(
                held.at[o], mem.at[zh, c, :, my_cols], ss.at[0], a_rs.at[back[n]], (o, c)
            ),
        )

    low = lax.broadcasted_iota(jnp.int32, (128, 128), 1) < HD

    def halves(top, bottom):
        return (
            jnp.where(low, top, roll64(bottom)).astype(BF),
            jnp.where(low, roll64(top), bottom).astype(BF),
        )

    def pack_heads(rows, out):
        for t in range(2):
            tile = slice(t * 128, (t + 1) * 128)
            out[2 * t], out[2 * t + 1] = halves(
                rows[0:128, tile].astype(F32), rows[128:256, tile].astype(F32)
            )

    def deal(out, into, which):
        for k in (2, 1, 3):
            h = (zh + k) % 4
            send(out.at[h], into.at[zh], ss.at[which], d_rs.at[which], at_seq(y, h, j))
        into[zh] = out[zh]

    def dealt(into, which):
        arrived(into.at[pl.ds(0, 3)], d_rs.at[which])

    loads[2].wait()
    pack_heads(qin, q_s)
    loads[3].wait()
    pack_heads(gin, g_s)

    loads[4].wait()
    loads[5].wait()
    low_w = lax.broadcasted_iota(jnp.int32, (256, 128), 1) < HD

    @pl.loop(0, 16)
    def _(i):
        rows = pl.ds(pl.multiple_of(i * 256, 256), 256)
        sub = pl.ds(pl.multiple_of(i // 4 * 256, 256), 256)
        for t in range(2):
            kt = wk[rows, t * 128 : (t + 1) * 128].astype(F32)
            vt = wv[rows, t * 128 : (t + 1) * 128].astype(F32)
            wp[i % 4, sub, 2 * t * 128 : (2 * t + 1) * 128] = jnp.where(low_w, kt, roll64(vt)).astype(BF)
            wp[i % 4, sub, (2 * t + 1) * 128 : (2 * t + 2) * 128] = jnp.where(
                low_w, roll64(kt), vt
            ).astype(BF)

    loads[1].wait()

    def col(xx, zz):
        return xx * 2 + zz

    x1, x2, x3, ol = (x + 1) % 4, (x + 2) % 4, (x + 3) % 4, 1 - zl

    def quarter(n):
        return (zh + near[n]) % 4

    def pass_on(p, n, which, to):
        here = mem.at[quarter(n), p]
        send(here, here, ss.at[4], b_rs.at[n, which], (s, to))

    def own_rows(n):
        if n:
            arrived(mem.at[quarter(n), c], a_rs.at[n])
        else:
            arrived(fo.at[pl.ds(0, 7)], a_rs.at[n])
        pass_on(c, n, 1, col(x2, zl))
        pass_on(c, n, 0, col(x, ol))
        pass_on(c, n, 2, col(x1, zl))
        pass_on(c, n, 2, col(x3, zl))

    def relay_near(n):
        arrived(mem.at[quarter(n), 0], b_rs.at[n, 0])
        pass_on(col(x, ol), n, 2, col(x1, zl))
        pass_on(col(x, ol), n, 2, col(x3, zl))

    def relay_far(n):
        arrived(mem.at[quarter(n), 0], b_rs.at[n, 1])
        pass_on(col(x2, zl), n, 2, col(x, ol))

    own_rows(0)
    own_rows(1)
    relay_near(0)
    own_rows(2)
    relay_near(1)
    own_rows(3)
    deal(q_s, q_r, 1)
    relay_far(0)
    relay_near(2)
    relay_far(1)
    relay_near(3)
    relay_far(2)
    relay_far(3)

    kv_new = jnp.zeros((128, 512), F32)
    for n in range(4):
        arrived(mem.at[quarter(n), pl.ds(0, 5)], b_rs.at[n, 2])
        kv_new = kv_new + mm(mem[quarter(n)].reshape(128, 1024), wp[quarter(n)])
    kv_new = kv_new.astype(BF)
    for h in range(4):
        kvl[h] = kv_new[:, h * 128 : (h + 1) * 128]

    def slot(jj, yy, zz):
        return kv.at[jj * 4 + yy, pl.ds(pl.multiple_of(zz * 128, 128), 128)]

    for k in (2, 1, 3):
        h = (zh + k) % 4
        send(kvl.at[h], slot(j, y, zh), ss.at[12], k_rs.at[4 - k], at_seq(y, h, j))
    slot(j, y, zh)[...] = kvl[zh]
    y1, y2, y3, oj = (y + 1) % 4, (y + 2) % 4, (y + 3) % 4, 1 - j

    def share(yy, zz, sem, to):
        send(slot(j, yy, zz), slot(j, yy, zz), ss.at[5], k_rs.at[sem], to)

    for n, k in enumerate(near):
        zz = (zh + k) % 4
        if k:
            arrived(slot(j, y, zz), k_rs.at[k])
        share(y, zz, 12, at_seq(y2, zh, j))
        share(y, zz, 4 + n, at_seq(y1, zh, j))
        share(y, zz, 8 + n, at_seq(y3, zh, j))
        share(y, zz, 13, at_seq(y, zh, oj))

    qt[HD:, :] = jnp.zeros((HD, 1024), BF)
    dealt(q_r, 1)
    for b in range(4):
        turned = q_r[b].astype(F32).T.astype(BF)
        qt[0:HD, b * 256 : b * 256 + 128] = turned[:HD]
        qt[0:HD, b * 256 + 128 : (b + 1) * 256] = turned[HD:]
    mx[...] = jnp.full((8, 1024), -jnp.inf, F32)
    ls[...] = jnp.zeros((8, 1024), F32)
    att[...] = jnp.zeros((HD, 1024), F32)

    def stage(body):
        @pl.loop(0, 1)
        def _(_):
            for b in range(4):
                body(slice(b * 256, (b + 1) * 256))

    def gather_values(ch, cols):
        att[:, cols] = att[:, cols] * shr[0:1, cols] + mm(kvt[ch, HD:, :], ex[ch, :, cols])

    def attend(ch, before):
        def score(cols):
            top = jnp.full((8, 256), -jnp.inf, F32)
            for r in range(2):
                rows = slice(r * 256, (r + 1) * 256)
                v = mm(kv[ch, rows, :], qt[:, cols])
                sc[rows, cols] = v
                top = jnp.maximum(top, v.reshape(32, 8, 256).max(axis=0))
            top = jnp.maximum(mx[0:1, cols], jnp.max(top, axis=0, keepdims=True))
            tops[ch, :, cols] = jnp.broadcast_to(top, (8, 256))

        def weigh(cols):
            if before is not None:
                gather_values(before, cols)
            top = tops[ch, 0:1, cols]
            shrink = jnp.exp2((mx[0:1, cols] - top) * EXP2_SCALE)
            mx[:, cols] = tops[ch, :, cols]
            shr[:, cols] = jnp.broadcast_to(shrink, (8, 256))
            total = ls[:, cols] * shrink
            for r in range(2):
                rows = slice(r * 256, (r + 1) * 256)
                e = jnp.exp2((sc[rows, cols] - top) * EXP2_SCALE)
                total = total + e.reshape(32, 8, 256).sum(axis=0)
                ex[ch, rows, cols] = e.astype(BF)
            ls[:, cols] = total

        for r in range(2):
            rows = slice(r * 256, (r + 1) * 256)
            kvt[ch, :, rows] = kv[ch, rows, :].astype(F32).T.astype(BF)
        stage(score)
        stage(weigh)

    attend(j * 4 + y, None)
    def forward(n):
        zz = (zh + near[n]) % 4
        arrived(slot(j, y3, zz), k_rs.at[4 + n])
        share(y3, zz, 16, at_seq(y, zh, oj))
        arrived(slot(j, y1, zz), k_rs.at[8 + n])
        share(y1, zz, 14, at_seq(y, zh, oj))

    forward(0)
    forward(1)
    arrived(kv.at[oj * 4 + y], k_rs.at[13])
    attend(oj * 4 + y, j * 4 + y)
    forward(2)
    forward(3)
    deal(g_s, g_r, 2)

    def chunk(t):
        k = jnp.where(t == 2, 3, jnp.where(t == 3, 1, 2))
        k = jnp.where(t == 5, 3, jnp.where(t == 6, 1, jnp.where(t == 1, 0, k)))
        own = (t == 2) | (t == 3) | (t == 4)
        return k, own, jnp.where(own, j, oj) * 4 + (y + k) % 4

    @pl.loop(2, 8)
    def _(i):
        k, own, now = chunk(i)

        @pl.when(i == 4)
        def _():
            far = kv.at[j * 4 + y2]
            arrived(far, k_rs.at[12])
            send(far, far, ss.at[5], k_rs.at[15], at_seq(y, zh, oj))

        @pl.when(jnp.logical_not(own))
        def _():
            arrived(kv.at[now], k_rs.at[13 + k])

        attend(now, chunk(i - 1)[2])

    stage(lambda cols: gather_values(oj * 4 + y2, cols))

    dealt(g_r, 2)
    gs[0:HD, :] = jnp.zeros((HD, 1024), BF)
    for b in range(4):
        cols = slice(b * 256, (b + 1) * 256)
        turned = g_r[b].astype(F32).T
        inv = 1.0 / jnp.sum(ls[:, cols], axis=0, keepdims=True)
        gt[:, b * 256 : b * 256 + 128] = turned[:HD] * inv[:, :128]
        gt[:, b * 256 + 128 : (b + 1) * 256] = turned[HD:] * inv[:, 128:]
        att[:, cols] = att[:, cols] * inv
    dqt[...] = jnp.zeros((HD, 1024), F32)

    def query_grad(ch, at, cols):
        dqt[:, cols] += mm(kvt[ch, 0:HD, :], ds[at, :, cols])

    def grads(ch, before, at):
        def score_grad(cols):
            query_grad(before, 1 - at, cols)
            shrink = jnp.exp2((tops[ch, 0:1, cols] - mx[0:1, cols]) * EXP2_SCALE)
            scaled = (gt[:, cols] * shrink).astype(BF)
            gs[HD:, cols] = scaled
            delta = jnp.sum(scaled.astype(F32) * att[:, cols], axis=0, keepdims=True)
            for r in range(2):
                rows = slice(r * 256, (r + 1) * 256)
                pg = mm(kv[ch, rows, :], gs[:, cols])
                ds[at, rows, cols] = (ex[ch, rows, cols].astype(F32) * (pg - delta)).astype(BF)

        stage(score_grad)
        dk = mm_t(qt[0:HD, :], ds[at]) * FACTOR
        dv = mm_t(gs[HD:, :], ex[ch])
        for zz in range(4):
            gk[zz, 0:HD, :] = dk[:, zz * 128 : (zz + 1) * 128]
            gk[zz, HD:, :] = dv[:, zz * 128 : (zz + 1) * 128]

    ds[1] = jnp.zeros((512, 1024), BF)

    at_kz = tuple((zh + k) % 4 for k in (2, 1, 3, 0))

    def turn(i):
        mine = (i == 2) | (i == 4) | (i == 5) | (i == 7)
        far = jnp.where(i < 4, jnp.where(i == 3, 3, jnp.where(i == 1, 1, 0)), 2)
        k = jnp.where(i == 4, 1, jnp.where(i == 5, 3, far))
        return mine, k, jnp.where(mine, j, oj) * 4 + (y + 2 + k) % 4

    @pl.loop(0, 8)
    def _(i):
        mine, k, now = turn(i)
        yy = (y + 2 + k) % 4
        grads(now, turn(jnp.maximum(i - 1, 0))[2], i % 2)

        @pl.when(jnp.logical_not(mine))
        def _():
            sb_s[k] = gk[...].astype(BF)
            send(sb_s.at[k], sb_r.at[k], ss.at[6], sb_rs.at[k], at_seq(y, zh, oj))

        @pl.when(mine)
        def _():
            arrived(sb_r.at[k], sb_rs.at[k])
            both = gk[...] + sb_r[k].astype(F32)

            @pl.when(k == 2)
            def _():
                tot[...] = both

            @pl.when(k != 2)
            def _():
                at = k - k // 3
                rs_s[at] = both.astype(BF)
                for n, zz in enumerate(at_kz):
                    send(
                        rs_s.at[at, zz], rs_r.at[at, zz], ss.at[11], r_rs.at[n],
                        at_seq(yy, zh, j),
                    )

    for n, zz in enumerate(at_kz):
        acc = tot[zz]
        arrived(rs_r.at[pl.ds(0, 3), 0], r_rs.at[n])
        for k in range(3):
            acc = acc + rs_r[k, zz].astype(F32)
        acc = acc.T
        if n < 3:
            k = (2, 1, 3)[n]
            zb_s[zz] = acc.astype(BF)
            send(zb_s.at[zz], hb.at[4 - k], ss.at[7], d_rs.at[8 - k], at_seq(y, zz, j))
        else:
            hb[0] = acc.astype(BF)

    stage(lambda cols: query_grad(j * 4 + y, 1, cols))
    for b in range(4):
        pair = [dqt[:, b * 256 + r * 128 : b * 256 + (r + 1) * 128] * FACTOR for r in range(2)]
        dq_s[b] = jnp.concatenate(pair, axis=0).T.astype(BF)

    far_first = (2, 3, 1, 0)

    def head_part(n, r, o):
        cols = pl.ds(pl.multiple_of((zh + o) % 4 * 128, 128), 128)
        return mm_t(hb[o], wp[(zh + far_first[n]) % 4, r * 512 : (r + 1) * 512, cols])

    for n in range(4):
        for r in range(2):
            pa[n, :, r * 512 : (r + 1) * 512] = head_part(n, r, 0)

    @pl.loop(0, 2)
    def _(i):
        o = 1 + 2 * i
        arrived(hb.at[o], d_rs.at[4 + o])
        for n in range(4):
            for r in range(2):
                pa[n, :, r * 512 : (r + 1) * 512] += head_part(n, r, o)

    arrived(hb.at[2], d_rs.at[6])

    def partial(n):
        for r in range(2):
            cols = slice(r * 512, (r + 1) * 512)
            part = pa[n, :, cols] + head_part(n, r, 2)
            pm[n, :, :, cols] = part.astype(BF).reshape(8, 16, 512)
        for i, (block, to) in enumerate((
            (col(x2, ol), col(x, ol)),
            (col(x1, ol), col(x1, zl)),
            (col(x3, ol), col(x3, zl)),
        )):
            send(pm.at[n, block], e1_r.at[n, i], ss.at[8], e_rs.at[n, (i + 1) // 2], (s, to))

    def combine(n):
        arrived(e1_r.at[n, 0], e_rs.at[n, 0])
        e2_s[n, 0] = (e1_r[n, 0].astype(F32) + pm[n, col(x2, zl)].astype(F32)).astype(BF)
        send(e2_s.at[n, 0], e2_r.at[n, 0], ss.at[9], e_rs.at[n, 2], (s, col(x2, zl)))
        arrived(e1_r.at[n, pl.ds(1, 2)], e_rs.at[n, 1])
        e2_s[n, 1] = (
            e1_r[n, 1].astype(F32) + e1_r[n, 2].astype(F32) + pm[n, col(x, ol)].astype(F32)
        ).astype(BF)
        send(e2_s.at[n, 1], e2_r.at[n, 1], ss.at[9], e_rs.at[n, 2], (s, col(x, ol)))
        for i, to in ((3, col(x1, zl)), (4, col(x3, zl))):
            send(pm.at[n, to], e1_r.at[n, i], ss.at[8], e_rs.at[n, 2], (s, to))

    def finish(n):
        acc = pm[n, c].astype(F32)
        arrived(e1_r.at[n, pl.ds(0, 4)], e_rs.at[n, 2])
        for i in range(2):
            acc = acc + e1_r[n, 3 + i].astype(F32) + e2_r[n, i].astype(F32)
        fs[n] = acc.astype(BF)
        feature_group(
            far_first[n],
            lambda o, cols: send(
                fs.at[n, :, cols], fo.at[s],
                ss.at[10], d_rs.at[4], (o, c),
            ),
        )

    for n in range(4):
        partial(n)
    deal(dq_s, dq_r, 3)
    combine(0)
    combine(1)
    finish(0)
    combine(2)
    finish(1)
    combine(3)

    finish(2)
    finish(3)
    dealt(dq_r, 3)
    for t in range(2):
        a = dq_r[2 * t].astype(F32)
        b = dq_r[2 * t + 1].astype(F32)
        tile = slice(t * 128, (t + 1) * 128)
        dq_out[0:128, tile], dq_out[128:256, tile] = halves(a, b)

    fo[s] = fs[3, :, my_cols]
    arrived(fo.at[pl.ds(0, 31)], d_rs.at[4])

    dm_out[...] = fo[...]

    for n, ref in enumerate((
        fo.at[pl.ds(0, 31)], kvl.at[pl.ds(0, 3)], kvl.at[pl.ds(0, 3)], kvl.at[pl.ds(0, 3)],
        mem.at[:, pl.ds(0, 7)], kv.at[pl.ds(0, 7)], sb_s, kvl.at[pl.ds(0, 3)],
        e1_r, e2_s, fo.at[pl.ds(0, 31)], rs_s, kvl.at[pl.ds(0, 3)],
    )):
        sent(ref, ss.at[n])


def local(memory, query, out_grad, w_key, w_value):
    dma = pltpu.SemaphoreType.DMA
    v = pltpu.VMEM
    dq, dm = pl.pallas_call(
        kernel,
        out_shape=(
            pltpu.VMEM((256, 256), BF),
            pltpu.VMEM((32, 16, 128), BF),
        ),
        in_specs=[pl.BlockSpec(memory_space=pl.ANY)] * 5,
        out_specs=(pl.BlockSpec(memory_space=pltpu.VMEM),) * 2,
        scratch_shapes=[
            v((32, 16, 128), BF),
            v((4096, 256), BF), v((4096, 256), BF), v((4, 1024, 512), BF),
            v((256, 256), BF), v((256, 256), BF),
            v((4, 8, 16, 1024), BF), v((4, 128, 128), BF),
            v((8, 512, 128), BF), v((8, 128, 512), BF),
            v((4, 128, 128), BF), v((4, 128, 128), BF), v((4, 128, 128), BF), v((4, 128, 128), BF),
            v((128, 1024), BF), v((HD, 1024), F32), v((128, 1024), BF),
            v((512, 1024), F32), v((8, 512, 1024), BF), v((2, 512, 1024), BF),
            v((8, 1024), F32), v((8, 8, 1024), F32), v((8, 1024), F32), v((8, 1024), F32), v((HD, 1024), F32),
            v((HD, 1024), F32), v((4, 128, 128), F32),
            v((4, 4, 128, 128), BF), v((4, 4, 128, 128), BF),
            v((3, 4, 128, 128), BF), v((3, 4, 128, 128), BF), v((4, 128, 128), F32),
            v((4, 128, 128), BF), v((4, 128, 128), BF), v((4, 128, 1024), F32),
            v((4, 128, 128), BF), v((4, 128, 128), BF),
            v((4, 8, 16, 1024), BF), v((4, 5, 16, 1024), BF),
            v((4, 2, 16, 1024), BF), v((4, 2, 16, 1024), BF),
            v((4, 16, 1024), BF), v((32, 16, 128), BF),
            dma((6,)), dma((13,)), dma((4,)), dma((4, 3)), dma((17,)), dma((4,)), dma((4,)),
            dma((8,)), dma((4, 3)),
        ],
        compiler_params=pltpu.CompilerParams(
            collective_id=0, has_side_effects=True, vmem_limit_bytes=60 * 1024 * 1024
        ),
    )(memory.reshape(32, 16, 128), query, out_grad, w_key, w_value)
    return pl.pallas_call(
        write_out,
        out_shape=(
            jax.ShapeDtypeStruct((256, 256), BF),
            jax.ShapeDtypeStruct((512, 128), BF),
        ),
        in_specs=[pl.BlockSpec(memory_space=pltpu.VMEM)] * 2,
        out_specs=(pl.BlockSpec(memory_space=pl.ANY),) * 2,
        scratch_shapes=[pltpu.SemaphoreType.DMA((2,))],
    )(
        pltpu.with_memory_space_constraint(dq, pltpu.VMEM),
        pltpu.with_memory_space_constraint(dm.reshape(512, 128), pltpu.VMEM),
    )


def write_out(dq_ref, dm_ref, dq_out, dm_out, sem):
    copies = [
        pltpu.make_async_copy(dq_ref, dq_out, sem.at[0]),
        pltpu.make_async_copy(dm_ref, dm_out, sem.at[1]),
    ]
    for copy in copies:
        copy.start()
    for copy in copies:
        copy.wait()


def solution(mesh):
    return jax.shard_map(
        local,
        mesh=mesh,
        in_specs=(
            P("col", "seq"),
            P("seq", "col"),
            P("seq", "col"),
            P(None, "col"),
            P(None, "col"),
        ),
        out_specs=(P("seq", "col"), P("col", "seq")),
        check_vma=False,
    )
```

```python
import math

import jax
import jax.numpy as jnp
from jax import lax
from jax.experimental import pallas as pl
from jax.experimental.pallas import tpu as pltpu
from jax.sharding import PartitionSpec as P

HD = 64
BF = jnp.bfloat16
F32 = jnp.float32
MESH = pl.DeviceIdType.MESH
EXP2_SCALE = math.log2(math.e) / math.sqrt(HD)
FACTOR = 1.0 / math.sqrt(HD)


def mm(a, b):
    return jnp.dot(a, b, preferred_element_type=F32)


def mm_t(a, b):
    return lax.dot_general(a, b, (((1,), (1,)), ((), ())), preferred_element_type=F32)


def roll64(a):
    return pltpu.roll(a, 64, 1)


def kernel(
    mem_hbm, q_hbm, g_hbm, wk_hbm, wv_hbm, dq_out, dm_out, held,
    wk, wv, wp, qin, gin, mem, kvl, kv, kvt, q_s, q_r, g_s, g_r, qt, gt, gs,
    sc, ex, ds, mx, tops, shr, ls, att, dqt, gk, sb_s, sb_r, rs_s, rs_r, tot, zb_s, hb, pa, dq_s, dq_r,
    pm, e1_r, e2_s, e2_r, fs, fo,
    in_sem, ss, a_rs, b_rs, k_rs, sb_rs, r_rs, d_rs, e_rs,
):
    s = lax.axis_index("seq")
    c = lax.axis_index("col")
    y, zh, j = s // 8, (s // 2) % 4, s % 2
    x, zl = c // 2, c % 2

    def at_seq(yy, zz, jj):
        return ((yy * 4 + zz) * 2 + jj, c)

    def send(src, dst, ss, rs, to):
        d = pltpu.make_async_remote_copy(
            src_ref=src, dst_ref=dst, send_sem=ss, recv_sem=rs,
            device_id=to, device_id_type=MESH,
        )
        d.start()
        return d

    def arrived(ref, rs):
        pltpu.make_async_remote_copy(
            src_ref=ref, dst_ref=ref, send_sem=rs, recv_sem=rs,
            device_id=(s, c), device_id_type=MESH,
        ).wait_recv()

    def sent(ref, ss):
        pltpu.make_async_remote_copy(
            src_ref=ref, dst_ref=ref, send_sem=ss, recv_sem=ss,
            device_id=(s, c), device_id_type=MESH,
        ).wait_send()

    barrier = pltpu.get_barrier_semaphore()

    @pl.loop(1, 32)
    def _(k):
        pl.semaphore_signal(barrier, inc=1, device_id=((s + k) % 32, c), device_id_type=MESH)

    @pl.loop(1, 8)
    def _(k):
        pl.semaphore_signal(barrier, inc=1, device_id=(s, (c + k) % 8), device_id_type=MESH)

    loads = [
        pltpu.make_async_copy(mem_hbm, held, in_sem.at[5]),
        pltpu.make_async_copy(
            mem_hbm.at[s],
            mem.at[zh, c, :, pl.ds(pl.multiple_of((y * 2 + j) * 128, 128), 128)],
            in_sem.at[4],
        ),
        pltpu.make_async_copy(q_hbm, qin, in_sem.at[0]),
        pltpu.make_async_copy(g_hbm, gin, in_sem.at[1]),
        pltpu.make_async_copy(wk_hbm, wk, in_sem.at[2]),
        pltpu.make_async_copy(wv_hbm, wv, in_sem.at[3]),
    ]
    for ld in loads:
        ld.start()

    loads[0].wait()
    pl.semaphore_wait(barrier, 38)

    my_cols = pl.ds(pl.multiple_of((y * 2 + j) * 128, 128), 128)
    near = (0, 1, 3, 2)

    def far_y(m):
        at = m // 2
        return jnp.where(at == 0, 2, jnp.where(at == 1, 1, jnp.where(at == 2, 3, 0)))

    def feature_group(dz, act):
        @pl.loop(0, 8 if dz else 7)
        def _(m):
            oy, oc = (y + far_y(m)) % 4, (j + 1 + m) % 2
            cols = pl.ds(pl.multiple_of((oy * 2 + oc) * 128, 128), 128)
            act((oy * 4 + (zh + dz) % 4) * 2 + oc, cols)

    back = (0, 2, 1, 3)
    for n in range(4):
        feature_group(
            near[n],
            lambda o, cols: send(
                held.at[o], mem.at[zh, c, :, my_cols], ss.at[0], a_rs.at[back[n]], (o, c)
            ),
        )

    low = lax.broadcasted_iota(jnp.int32, (128, 128), 1) < HD

    def halves(top, bottom):
        return (
            jnp.where(low, top, roll64(bottom)).astype(BF),
            jnp.where(low, roll64(top), bottom).astype(BF),
        )

    def pack_heads(rows, out):
        for t in range(2):
            tile = slice(t * 128, (t + 1) * 128)
            out[2 * t], out[2 * t + 1] = halves(
                rows[0:128, tile].astype(F32), rows[128:256, tile].astype(F32)
            )

    def deal(out, into, which):
        for k in (2, 1, 3):
            h = (zh + k) % 4
            send(out.at[h], into.at[zh], ss.at[which], d_rs.at[which], at_seq(y, h, j))
        into[zh] = out[zh]

    def dealt(into, which):
        arrived(into.at[pl.ds(0, 3)], d_rs.at[which])

    loads[2].wait()
    pack_heads(qin, q_s)
    loads[3].wait()
    pack_heads(gin, g_s)

    loads[4].wait()
    loads[5].wait()
    low_w = lax.broadcasted_iota(jnp.int32, (256, 128), 1) < HD

    @pl.loop(0, 16)
    def _(i):
        rows = pl.ds(pl.multiple_of(i * 256, 256), 256)
        sub = pl.ds(pl.multiple_of(i // 4 * 256, 256), 256)
        for t in range(2):
            kt = wk[rows, t * 128 : (t + 1) * 128].astype(F32)
            vt = wv[rows, t * 128 : (t + 1) * 128].astype(F32)
            wp[i % 4, sub, 2 * t * 128 : (2 * t + 1) * 128] = jnp.where(low_w, kt, roll64(vt)).astype(BF)
            wp[i % 4, sub, (2 * t + 1) * 128 : (2 * t + 2) * 128] = jnp.where(
                low_w, roll64(kt), vt
            ).astype(BF)

    loads[1].wait()

    def col(xx, zz):
        return xx * 2 + zz

    x1, x2, x3, ol = (x + 1) % 4, (x + 2) % 4, (x + 3) % 4, 1 - zl

    def quarter(n):
        return (zh + near[n]) % 4

    def pass_on(p, n, which, to):
        here = mem.at[quarter(n), p]
        send(here, here, ss.at[4], b_rs.at[n, which], (s, to))

    def own_rows(n):
        if n:
            arrived(mem.at[quarter(n), c], a_rs.at[n])
        else:
            arrived(fo.at[pl.ds(0, 7)], a_rs.at[n])
        pass_on(c, n, 1, col(x2, zl))
        pass_on(c, n, 0, col(x, ol))
        pass_on(c, n, 2, col(x1, zl))
        pass_on(c, n, 2, col(x3, zl))

    def relay_near(n):
        arrived(mem.at[quarter(n), 0], b_rs.at[n, 0])
        pass_on(col(x, ol), n, 2, col(x1, zl))
        pass_on(col(x, ol), n, 2, col(x3, zl))

    def relay_far(n):
        arrived(mem.at[quarter(n), 0], b_rs.at[n, 1])
        pass_on(col(x2, zl), n, 2, col(x, ol))

    own_rows(0)
    own_rows(1)
    relay_near(0)
    own_rows(2)
    relay_near(1)
    relay_far(0)
    own_rows(3)
    deal(q_s, q_r, 1)
    relay_near(2)
    relay_far(1)
    relay_far(2)
    relay_near(3)
    relay_far(3)

    kv_new = jnp.zeros((128, 512), F32)
    for n in range(4):
        arrived(mem.at[quarter(n), pl.ds(0, 5)], b_rs.at[n, 2])
        kv_new = kv_new + mm(mem[quarter(n)].reshape(128, 1024), wp[quarter(n)])
    kv_new = kv_new.astype(BF)
    for h in range(4):
        kvl[h] = kv_new[:, h * 128 : (h + 1) * 128]

    def slot(jj, yy, zz):
        return kv.at[jj * 4 + yy, pl.ds(pl.multiple_of(zz * 128, 128), 128)]

    for k in (2, 1, 3):
        h = (zh + k) % 4
        send(kvl.at[h], slot(j, y, zh), ss.at[12], k_rs.at[4 - k], at_seq(y, h, j))
    slot(j, y, zh)[...] = kvl[zh]
    y1, y2, y3, oj = (y + 1) % 4, (y + 2) % 4, (y + 3) % 4, 1 - j

    def share(yy, zz, sem, to):
        send(slot(j, yy, zz), slot(j, yy, zz), ss.at[5], k_rs.at[sem], to)

    for n, k in enumerate(near):
        zz = (zh + k) % 4
        if k:
            arrived(slot(j, y, zz), k_rs.at[k])
        share(y, zz, 12, at_seq(y2, zh, j))
        share(y, zz, 4 + n, at_seq(y1, zh, j))
        share(y, zz, 8 + n, at_seq(y3, zh, j))
        share(y, zz, 13, at_seq(y, zh, oj))

    qt[HD:, :] = jnp.zeros((HD, 1024), BF)
    dealt(q_r, 1)
    for b in range(4):
        turned = q_r[b].astype(F32).T.astype(BF)
        qt[0:HD, b * 256 : b * 256 + 128] = turned[:HD]
        qt[0:HD, b * 256 + 128 : (b + 1) * 256] = turned[HD:]
    mx[...] = jnp.full((8, 1024), -jnp.inf, F32)
    ls[...] = jnp.zeros((8, 1024), F32)
    att[...] = jnp.zeros((HD, 1024), F32)

    def stage(body):
        @pl.loop(0, 1)
        def _(_):
            for b in range(4):
                body(slice(b * 256, (b + 1) * 256))

    def gather_values(ch, cols):
        att[:, cols] = att[:, cols] * shr[0:1, cols] + mm(kvt[ch, HD:, :], ex[ch, :, cols])

    def attend(ch, before):
        def score(cols):
            top = jnp.full((8, 256), -jnp.inf, F32)
            for r in range(2):
                rows = slice(r * 256, (r + 1) * 256)
                v = mm(kv[ch, rows, :], qt[:, cols])
                sc[rows, cols] = v
                top = jnp.maximum(top, v.reshape(32, 8, 256).max(axis=0))
            top = jnp.maximum(mx[0:1, cols], jnp.max(top, axis=0, keepdims=True))
            tops[ch, :, cols] = jnp.broadcast_to(top, (8, 256))

        def weigh(cols):
            if before is not None:
                gather_values(before, cols)
            top = tops[ch, 0:1, cols]
            shrink = jnp.exp2((mx[0:1, cols] - top) * EXP2_SCALE)
            mx[:, cols] = tops[ch, :, cols]
            shr[:, cols] = jnp.broadcast_to(shrink, (8, 256))
            total = ls[:, cols] * shrink
            for r in range(2):
                rows = slice(r * 256, (r + 1) * 256)
                e = jnp.exp2((sc[rows, cols] - top) * EXP2_SCALE)
                total = total + e.reshape(32, 8, 256).sum(axis=0)
                ex[ch, rows, cols] = e.astype(BF)
            ls[:, cols] = total

        for r in range(2):
            rows = slice(r * 256, (r + 1) * 256)
            kvt[ch, :, rows] = kv[ch, rows, :].astype(F32).T.astype(BF)
        stage(score)
        stage(weigh)

    attend(j * 4 + y, None)
    def forward(n):
        zz = (zh + near[n]) % 4
        arrived(slot(j, y3, zz), k_rs.at[4 + n])
        share(y3, zz, 16, at_seq(y, zh, oj))
        arrived(slot(j, y1, zz), k_rs.at[8 + n])
        share(y1, zz, 14, at_seq(y, zh, oj))

    forward(0)
    forward(1)
    arrived(kv.at[oj * 4 + y], k_rs.at[13])
    attend(oj * 4 + y, j * 4 + y)
    forward(2)
    forward(3)
    deal(g_s, g_r, 2)

    def chunk(t):
        k = jnp.where(t == 2, 3, jnp.where(t == 3, 1, 2))
        k = jnp.where(t == 5, 3, jnp.where(t == 6, 1, jnp.where(t == 1, 0, k)))
        own = (t == 2) | (t == 3) | (t == 4)
        return k, own, jnp.where(own, j, oj) * 4 + (y + k) % 4

    @pl.loop(2, 8)
    def _(i):
        k, own, now = chunk(i)

        @pl.when(i == 4)
        def _():
            far = kv.at[j * 4 + y2]
            arrived(far, k_rs.at[12])
            send(far, far, ss.at[5], k_rs.at[15], at_seq(y, zh, oj))

        @pl.when(jnp.logical_not(own))
        def _():
            arrived(kv.at[now], k_rs.at[13 + k])

        attend(now, chunk(i - 1)[2])

    stage(lambda cols: gather_values(oj * 4 + y2, cols))

    dealt(g_r, 2)
    gs[0:HD, :] = jnp.zeros((HD, 1024), BF)
    for b in range(4):
        cols = slice(b * 256, (b + 1) * 256)
        turned = g_r[b].astype(F32).T
        inv = 1.0 / jnp.sum(ls[:, cols], axis=0, keepdims=True)
        gt[:, b * 256 : b * 256 + 128] = turned[:HD] * inv[:, :128]
        gt[:, b * 256 + 128 : (b + 1) * 256] = turned[HD:] * inv[:, 128:]
        att[:, cols] = att[:, cols] * inv
    dqt[...] = jnp.zeros((HD, 1024), F32)

    def query_grad(ch, at, cols):
        dqt[:, cols] += mm(kvt[ch, 0:HD, :], ds[at, :, cols])

    def grads(ch, before, at):
        def score_grad(cols):
            query_grad(before, 1 - at, cols)
            shrink = jnp.exp2((tops[ch, 0:1, cols] - mx[0:1, cols]) * EXP2_SCALE)
            scaled = (gt[:, cols] * shrink).astype(BF)
            gs[HD:, cols] = scaled
            delta = jnp.sum(scaled.astype(F32) * att[:, cols], axis=0, keepdims=True)
            for r in range(2):
                rows = slice(r * 256, (r + 1) * 256)
                pg = mm(kv[ch, rows, :], gs[:, cols])
                ds[at, rows, cols] = (ex[ch, rows, cols].astype(F32) * (pg - delta)).astype(BF)

        stage(score_grad)
        dk = mm_t(qt[0:HD, :], ds[at]) * FACTOR
        dv = mm_t(gs[HD:, :], ex[ch])
        for zz in range(4):
            gk[zz, 0:HD, :] = dk[:, zz * 128 : (zz + 1) * 128]
            gk[zz, HD:, :] = dv[:, zz * 128 : (zz + 1) * 128]

    ds[1] = jnp.zeros((512, 1024), BF)

    at_kz = tuple((zh + k) % 4 for k in (2, 1, 3, 0))

    def turn(i):
        mine = (i == 2) | (i == 4) | (i == 5) | (i == 7)
        far = jnp.where(i < 4, jnp.where(i == 3, 3, jnp.where(i == 1, 1, 0)), 2)
        k = jnp.where(i == 4, 1, jnp.where(i == 5, 3, far))
        return mine, k, jnp.where(mine, j, oj) * 4 + (y + 2 + k) % 4

    @pl.loop(0, 8)
    def _(i):
        mine, k, now = turn(i)
        yy = (y + 2 + k) % 4
        grads(now, turn(jnp.maximum(i - 1, 0))[2], i % 2)

        @pl.when(jnp.logical_not(mine))
        def _():
            sb_s[k] = gk[...].astype(BF)
            send(sb_s.at[k], sb_r.at[k], ss.at[6], sb_rs.at[k], at_seq(y, zh, oj))

        @pl.when(mine)
        def _():
            arrived(sb_r.at[k], sb_rs.at[k])
            both = gk[...] + sb_r[k].astype(F32)

            @pl.when(k == 2)
            def _():
                tot[...] = both

            @pl.when(k != 2)
            def _():
                at = k - k // 3
                rs_s[at] = both.astype(BF)
                for n, zz in enumerate(at_kz):
                    send(
                        rs_s.at[at, zz], rs_r.at[at, zz], ss.at[11], r_rs.at[n],
                        at_seq(yy, zh, j),
                    )

    for n, zz in enumerate(at_kz):
        acc = tot[zz]
        arrived(rs_r.at[pl.ds(0, 3), 0], r_rs.at[n])
        for k in range(3):
            acc = acc + rs_r[k, zz].astype(F32)
        acc = acc.T
        if n < 3:
            k = (2, 1, 3)[n]
            zb_s[zz] = acc.astype(BF)
            send(zb_s.at[zz], hb.at[4 - k], ss.at[7], d_rs.at[8 - k], at_seq(y, zz, j))
        else:
            hb[0] = acc.astype(BF)

    stage(lambda cols: query_grad(j * 4 + y, 1, cols))
    for b in range(4):
        pair = [dqt[:, b * 256 + r * 128 : b * 256 + (r + 1) * 128] * FACTOR for r in range(2)]
        dq_s[b] = jnp.concatenate(pair, axis=0).T.astype(BF)

    far_first = (2, 3, 1, 0)

    def head_part(n, r, o):
        cols = pl.ds(pl.multiple_of((zh + o) % 4 * 128, 128), 128)
        return mm_t(hb[o], wp[(zh + far_first[n]) % 4, r * 512 : (r + 1) * 512, cols])

    for n in range(4):
        for r in range(2):
            pa[n, :, r * 512 : (r + 1) * 512] = head_part(n, r, 0)

    @pl.loop(0, 2)
    def _(i):
        o = 1 + 2 * i
        arrived(hb.at[o], d_rs.at[4 + o])
        for n in range(4):
            for r in range(2):
                pa[n, :, r * 512 : (r + 1) * 512] += head_part(n, r, o)

    arrived(hb.at[2], d_rs.at[6])

    def partial(n):
        for r in range(2):
            cols = slice(r * 512, (r + 1) * 512)
            part = pa[n, :, cols] + head_part(n, r, 2)
            pm[n, :, :, cols] = part.astype(BF).reshape(8, 16, 512)
        for i, (block, to) in enumerate((
            (col(x2, ol), col(x, ol)),
            (col(x1, ol), col(x1, zl)),
            (col(x3, ol), col(x3, zl)),
        )):
            send(pm.at[n, block], e1_r.at[n, i], ss.at[8], e_rs.at[n, (i + 1) // 2], (s, to))

    def combine(n):
        arrived(e1_r.at[n, 0], e_rs.at[n, 0])
        e2_s[n, 0] = (e1_r[n, 0].astype(F32) + pm[n, col(x2, zl)].astype(F32)).astype(BF)
        send(e2_s.at[n, 0], e2_r.at[n, 0], ss.at[9], e_rs.at[n, 2], (s, col(x2, zl)))
        arrived(e1_r.at[n, pl.ds(1, 2)], e_rs.at[n, 1])
        e2_s[n, 1] = (
            e1_r[n, 1].astype(F32) + e1_r[n, 2].astype(F32) + pm[n, col(x, ol)].astype(F32)
        ).astype(BF)
        send(e2_s.at[n, 1], e2_r.at[n, 1], ss.at[9], e_rs.at[n, 2], (s, col(x, ol)))
        for i, to in ((3, col(x1, zl)), (4, col(x3, zl))):
            send(pm.at[n, to], e1_r.at[n, i], ss.at[8], e_rs.at[n, 2], (s, to))

    def finish(n):
        acc = pm[n, c].astype(F32)
        arrived(e1_r.at[n, pl.ds(0, 4)], e_rs.at[n, 2])
        for i in range(2):
            acc = acc + e1_r[n, 3 + i].astype(F32) + e2_r[n, i].astype(F32)
        fs[n] = acc.astype(BF)
        feature_group(
            far_first[n],
            lambda o, cols: send(
                fs.at[n, :, cols], fo.at[s],
                ss.at[10], d_rs.at[4], (o, c),
            ),
        )

    for n in range(4):
        partial(n)
    for n in range(4):
        combine(n)
    deal(dq_s, dq_r, 3)
    finish(0)
    finish(1)
    finish(2)
    finish(3)
    dealt(dq_r, 3)
    for t in range(2):
        a = dq_r[2 * t].astype(F32)
        b = dq_r[2 * t + 1].astype(F32)
        tile = slice(t * 128, (t + 1) * 128)
        dq_out[0:128, tile], dq_out[128:256, tile] = halves(a, b)

    fo[s] = fs[3, :, my_cols]
    arrived(fo.at[pl.ds(0, 31)], d_rs.at[4])

    dm_out[...] = fo[...]

    for n, ref in enumerate((
        fo.at[pl.ds(0, 31)], kvl.at[pl.ds(0, 3)], kvl.at[pl.ds(0, 3)], kvl.at[pl.ds(0, 3)],
        mem.at[:, pl.ds(0, 7)], kv.at[pl.ds(0, 7)], sb_s, kvl.at[pl.ds(0, 3)],
        e1_r, e2_s, fo.at[pl.ds(0, 31)], rs_s, kvl.at[pl.ds(0, 3)],
    )):
        sent(ref, ss.at[n])


def local(memory, query, out_grad, w_key, w_value):
    dma = pltpu.SemaphoreType.DMA
    v = pltpu.VMEM
    dq, dm = pl.pallas_call(
        kernel,
        out_shape=(
            pltpu.VMEM((256, 256), BF),
            pltpu.VMEM((32, 16, 128), BF),
        ),
        in_specs=[pl.BlockSpec(memory_space=pl.ANY)] * 5,
        out_specs=(pl.BlockSpec(memory_space=pltpu.VMEM),) * 2,
        scratch_shapes=[
            v((32, 16, 128), BF),
            v((4096, 256), BF), v((4096, 256), BF), v((4, 1024, 512), BF),
            v((256, 256), BF), v((256, 256), BF),
            v((4, 8, 16, 1024), BF), v((4, 128, 128), BF),
            v((8, 512, 128), BF), v((8, 128, 512), BF),
            v((4, 128, 128), BF), v((4, 128, 128), BF), v((4, 128, 128), BF), v((4, 128, 128), BF),
            v((128, 1024), BF), v((HD, 1024), F32), v((128, 1024), BF),
            v((512, 1024), F32), v((8, 512, 1024), BF), v((2, 512, 1024), BF),
            v((8, 1024), F32), v((8, 8, 1024), F32), v((8, 1024), F32), v((8, 1024), F32), v((HD, 1024), F32),
            v((HD, 1024), F32), v((4, 128, 128), F32),
            v((4, 4, 128, 128), BF), v((4, 4, 128, 128), BF),
            v((3, 4, 128, 128), BF), v((3, 4, 128, 128), BF), v((4, 128, 128), F32),
            v((4, 128, 128), BF), v((4, 128, 128), BF), v((4, 128, 1024), F32),
            v((4, 128, 128), BF), v((4, 128, 128), BF),
            v((4, 8, 16, 1024), BF), v((4, 5, 16, 1024), BF),
            v((4, 2, 16, 1024), BF), v((4, 2, 16, 1024), BF),
            v((4, 16, 1024), BF), v((32, 16, 128), BF),
            dma((6,)), dma((13,)), dma((4,)), dma((4, 3)), dma((17,)), dma((4,)), dma((4,)),
            dma((8,)), dma((4, 3)),
        ],
        compiler_params=pltpu.CompilerParams(
            collective_id=0, has_side_effects=True, vmem_limit_bytes=60 * 1024 * 1024
        ),
    )(memory.reshape(32, 16, 128), query, out_grad, w_key, w_value)
    return pl.pallas_call(
        write_out,
        out_shape=(
            jax.ShapeDtypeStruct((256, 256), BF),
            jax.ShapeDtypeStruct((512, 128), BF),
        ),
        in_specs=[pl.BlockSpec(memory_space=pltpu.VMEM)] * 2,
        out_specs=(pl.BlockSpec(memory_space=pl.ANY),) * 2,
        scratch_shapes=[pltpu.SemaphoreType.DMA((2,))],
    )(
        pltpu.with_memory_space_constraint(dq, pltpu.VMEM),
        pltpu.with_memory_space_constraint(dm.reshape(512, 128), pltpu.VMEM),
    )


def write_out(dq_ref, dm_ref, dq_out, dm_out, sem):
    copies = [
        pltpu.make_async_copy(dq_ref, dq_out, sem.at[0]),
        pltpu.make_async_copy(dm_ref, dm_out, sem.at[1]),
    ]
    for copy in copies:
        copy.start()
    for copy in copies:
        copy.wait()


def solution(mesh):
    return jax.shard_map(
        local,
        mesh=mesh,
        in_specs=(
            P("col", "seq"),
            P("seq", "col"),
            P("seq", "col"),
            P(None, "col"),
            P(None, "col"),
        ),
        out_specs=(P("seq", "col"), P("col", "seq")),
        check_vma=False,
    )
```

```python
import math

import jax
import jax.numpy as jnp
from jax import lax
from jax.experimental import pallas as pl
from jax.experimental.pallas import tpu as pltpu
from jax.sharding import PartitionSpec as P

HD = 64
BF = jnp.bfloat16
F32 = jnp.float32
MESH = pl.DeviceIdType.MESH
EXP2_SCALE = math.log2(math.e) / math.sqrt(HD)
FACTOR = 1.0 / math.sqrt(HD)


def mm(a, b):
    return jnp.dot(a, b, preferred_element_type=F32)


def mm_t(a, b):
    return lax.dot_general(a, b, (((1,), (1,)), ((), ())), preferred_element_type=F32)


def roll64(a):
    return pltpu.roll(a, 64, 1)


def kernel(
    mem_hbm, q_hbm, g_hbm, wk_hbm, wv_hbm, dq_out, dm_out, held,
    wk, wv, wp, qin, gin, mem, kvl, kv, kvt, q_s, q_r, g_s, g_r, qt, gt, gs,
    sc, ex, ds, mx, tops, shr, ls, att, dqt, gk, sb_s, sb_r, rs_s, rs_r, tot, zb_s, hb, pa, dq_s, dq_r,
    pm, e1_r, e2_s, e2_r, fs, fo,
    in_sem, ss, a_rs, b_rs, k_rs, sb_rs, r_rs, d_rs, e_rs,
):
    s = lax.axis_index("seq")
    c = lax.axis_index("col")
    y, zh, j = s // 8, (s // 2) % 4, s % 2
    x, zl = c // 2, c % 2

    def at_seq(yy, zz, jj):
        return ((yy * 4 + zz) * 2 + jj, c)

    def send(src, dst, ss, rs, to):
        d = pltpu.make_async_remote_copy(
            src_ref=src, dst_ref=dst, send_sem=ss, recv_sem=rs,
            device_id=to, device_id_type=MESH,
        )
        d.start()
        return d

    def arrived(ref, rs):
        pltpu.make_async_remote_copy(
            src_ref=ref, dst_ref=ref, send_sem=rs, recv_sem=rs,
            device_id=(s, c), device_id_type=MESH,
        ).wait_recv()

    def sent(ref, ss):
        pltpu.make_async_remote_copy(
            src_ref=ref, dst_ref=ref, send_sem=ss, recv_sem=ss,
            device_id=(s, c), device_id_type=MESH,
        ).wait_send()

    barrier = pltpu.get_barrier_semaphore()

    @pl.loop(1, 32)
    def _(k):
        pl.semaphore_signal(barrier, inc=1, device_id=((s + k) % 32, c), device_id_type=MESH)

    @pl.loop(1, 8)
    def _(k):
        pl.semaphore_signal(barrier, inc=1, device_id=(s, (c + k) % 8), device_id_type=MESH)

    loads = [
        pltpu.make_async_copy(mem_hbm, held, in_sem.at[5]),
        pltpu.make_async_copy(
            mem_hbm.at[s],
            mem.at[zh, c, :, pl.ds(pl.multiple_of((y * 2 + j) * 128, 128), 128)],
            in_sem.at[4],
        ),
        pltpu.make_async_copy(q_hbm, qin, in_sem.at[0]),
        pltpu.make_async_copy(g_hbm, gin, in_sem.at[1]),
        pltpu.make_async_copy(wk_hbm, wk, in_sem.at[2]),
        pltpu.make_async_copy(wv_hbm, wv, in_sem.at[3]),
    ]
    for ld in loads:
        ld.start()

    loads[0].wait()
    pl.semaphore_wait(barrier, 38)

    my_cols = pl.ds(pl.multiple_of((y * 2 + j) * 128, 128), 128)
    near = (0, 1, 3, 2)

    def far_y(m):
        at = m // 2
        return jnp.where(at == 0, 2, jnp.where(at == 1, 1, jnp.where(at == 2, 3, 0)))

    def feature_group(dz, act):
        @pl.loop(0, 8 if dz else 7)
        def _(m):
            oy, oc = (y + far_y(m)) % 4, (j + 1 + m) % 2
            cols = pl.ds(pl.multiple_of((oy * 2 + oc) * 128, 128), 128)
            act((oy * 4 + (zh + dz) % 4) * 2 + oc, cols)

    back = (0, 2, 1, 3)
    for n in range(4):
        feature_group(
            near[n],
            lambda o, cols: send(
                held.at[o], mem.at[zh, c, :, my_cols], ss.at[0], a_rs.at[back[n]], (o, c)
            ),
        )

    low = lax.broadcasted_iota(jnp.int32, (128, 128), 1) < HD

    def halves(top, bottom):
        return (
            jnp.where(low, top, roll64(bottom)).astype(BF),
            jnp.where(low, roll64(top), bottom).astype(BF),
        )

    def pack_heads(rows, out):
        for t in range(2):
            tile = slice(t * 128, (t + 1) * 128)
            out[2 * t], out[2 * t + 1] = halves(
                rows[0:128, tile].astype(F32), rows[128:256, tile].astype(F32)
            )

    def deal(out, into, which):
        for k in (2, 1, 3):
            h = (zh + k) % 4
            send(out.at[h], into.at[zh], ss.at[which], d_rs.at[which], at_seq(y, h, j))
        into[zh] = out[zh]

    def dealt(into, which):
        arrived(into.at[pl.ds(0, 3)], d_rs.at[which])

    loads[2].wait()
    pack_heads(qin, q_s)
    loads[3].wait()
    pack_heads(gin, g_s)

    loads[4].wait()
    loads[5].wait()
    low_w = lax.broadcasted_iota(jnp.int32, (256, 128), 1) < HD

    @pl.loop(0, 16)
    def _(i):
        rows = pl.ds(pl.multiple_of(i * 256, 256), 256)
        sub = pl.ds(pl.multiple_of(i // 4 * 256, 256), 256)
        for t in range(2):
            kt = wk[rows, t * 128 : (t + 1) * 128].astype(F32)
            vt = wv[rows, t * 128 : (t + 1) * 128].astype(F32)
            wp[i % 4, sub, 2 * t * 128 : (2 * t + 1) * 128] = jnp.where(low_w, kt, roll64(vt)).astype(BF)
            wp[i % 4, sub, (2 * t + 1) * 128 : (2 * t + 2) * 128] = jnp.where(
                low_w, roll64(kt), vt
            ).astype(BF)

    loads[1].wait()

    def col(xx, zz):
        return xx * 2 + zz

    x1, x2, x3, ol = (x + 1) % 4, (x + 2) % 4, (x + 3) % 4, 1 - zl

    def quarter(n):
        return (zh + near[n]) % 4

    def pass_on(p, n, which, to):
        here = mem.at[quarter(n), p]
        send(here, here, ss.at[4], b_rs.at[n, which], (s, to))

    def own_rows(n):
        if n:
            arrived(mem.at[quarter(n), c], a_rs.at[n])
        else:
            arrived(fo.at[pl.ds(0, 7)], a_rs.at[n])
        pass_on(c, n, 1, col(x2, zl))
        pass_on(c, n, 0, col(x, ol))
        pass_on(c, n, 2, col(x1, zl))
        pass_on(c, n, 2, col(x3, zl))

    def relay_near(n):
        arrived(mem.at[quarter(n), 0], b_rs.at[n, 0])
        pass_on(col(x, ol), n, 2, col(x1, zl))
        pass_on(col(x, ol), n, 2, col(x3, zl))

    def relay_far(n):
        arrived(mem.at[quarter(n), 0], b_rs.at[n, 1])
        pass_on(col(x2, zl), n, 2, col(x, ol))

    own_rows(0)
    own_rows(1)
    relay_near(0)
    own_rows(2)
    relay_near(1)
    relay_far(0)
    own_rows(3)
    relay_near(2)
    relay_far(1)
    deal(q_s, q_r, 1)
    relay_far(2)
    relay_near(3)
    relay_far(3)

    kv_new = jnp.zeros((128, 512), F32)
    for n in range(4):
        arrived(mem.at[quarter(n), pl.ds(0, 5)], b_rs.at[n, 2])
        kv_new = kv_new + mm(mem[quarter(n)].reshape(128, 1024), wp[quarter(n)])
    kv_new = kv_new.astype(BF)
    for h in range(4):
        kvl[h] = kv_new[:, h * 128 : (h + 1) * 128]

    def slot(jj, yy, zz):
        return kv.at[jj * 4 + yy, pl.ds(pl.multiple_of(zz * 128, 128), 128)]

    for k in (2, 1, 3):
        h = (zh + k) % 4
        send(kvl.at[h], slot(j, y, zh), ss.at[12], k_rs.at[4 - k], at_seq(y, h, j))
    slot(j, y, zh)[...] = kvl[zh]
    y1, y2, y3, oj = (y + 1) % 4, (y + 2) % 4, (y + 3) % 4, 1 - j

    def share(yy, zz, sem, to):
        send(slot(j, yy, zz), slot(j, yy, zz), ss.at[5], k_rs.at[sem], to)

    for n, k in enumerate(near):
        zz = (zh + k) % 4
        if k:
            arrived(slot(j, y, zz), k_rs.at[k])
        share(y, zz, 12, at_seq(y2, zh, j))
        share(y, zz, 4 + n, at_seq(y1, zh, j))
        share(y, zz, 8 + n, at_seq(y3, zh, j))
        share(y, zz, 13, at_seq(y, zh, oj))

    qt[HD:, :] = jnp.zeros((HD, 1024), BF)
    dealt(q_r, 1)
    for b in range(4):
        turned = q_r[b].astype(F32).T.astype(BF)
        qt[0:HD, b * 256 : b * 256 + 128] = turned[:HD]
        qt[0:HD, b * 256 + 128 : (b + 1) * 256] = turned[HD:]
    mx[...] = jnp.full((8, 1024), -jnp.inf, F32)
    ls[...] = jnp.zeros((8, 1024), F32)
    att[...] = jnp.zeros((HD, 1024), F32)

    def stage(body):
        @pl.loop(0, 1)
        def _(_):
            for b in range(4):
                body(slice(b * 256, (b + 1) * 256))

    def gather_values(ch, cols):
        att[:, cols] = att[:, cols] * shr[0:1, cols] + mm(kvt[ch, HD:, :], ex[ch, :, cols])

    def attend(ch, before):
        def score(cols):
            top = jnp.full((8, 256), -jnp.inf, F32)
            for r in range(2):
                rows = slice(r * 256, (r + 1) * 256)
                v = mm(kv[ch, rows, :], qt[:, cols])
                sc[rows, cols] = v
                top = jnp.maximum(top, v.reshape(32, 8, 256).max(axis=0))
            top = jnp.maximum(mx[0:1, cols], jnp.max(top, axis=0, keepdims=True))
            tops[ch, :, cols] = jnp.broadcast_to(top, (8, 256))

        def weigh(cols):
            if before is not None:
                gather_values(before, cols)
            top = tops[ch, 0:1, cols]
            shrink = jnp.exp2((mx[0:1, cols] - top) * EXP2_SCALE)
            mx[:, cols] = tops[ch, :, cols]
            shr[:, cols] = jnp.broadcast_to(shrink, (8, 256))
            total = ls[:, cols] * shrink
            for r in range(2):
                rows = slice(r * 256, (r + 1) * 256)
                e = jnp.exp2((sc[rows, cols] - top) * EXP2_SCALE)
                total = total + e.reshape(32, 8, 256).sum(axis=0)
                ex[ch, rows, cols] = e.astype(BF)
            ls[:, cols] = total

        for r in range(2):
            rows = slice(r * 256, (r + 1) * 256)
            kvt[ch, :, rows] = kv[ch, rows, :].astype(F32).T.astype(BF)
        stage(score)
        stage(weigh)

    attend(j * 4 + y, None)
    def forward(n):
        zz = (zh + near[n]) % 4
        arrived(slot(j, y3, zz), k_rs.at[4 + n])
        share(y3, zz, 16, at_seq(y, zh, oj))
        arrived(slot(j, y1, zz), k_rs.at[8 + n])
        share(y1, zz, 14, at_seq(y, zh, oj))

    forward(0)
    forward(1)
    arrived(kv.at[oj * 4 + y], k_rs.at[13])
    attend(oj * 4 + y, j * 4 + y)
    forward(2)
    forward(3)
    deal(g_s, g_r, 2)

    def chunk(t):
        k = jnp.where(t == 2, 3, jnp.where(t == 3, 1, 2))
        k = jnp.where(t == 5, 3, jnp.where(t == 6, 1, jnp.where(t == 1, 0, k)))
        own = (t == 2) | (t == 3) | (t == 4)
        return k, own, jnp.where(own, j, oj) * 4 + (y + k) % 4

    @pl.loop(2, 8)
    def _(i):
        k, own, now = chunk(i)

        @pl.when(i == 4)
        def _():
            far = kv.at[j * 4 + y2]
            arrived(far, k_rs.at[12])
            send(far, far, ss.at[5], k_rs.at[15], at_seq(y, zh, oj))

        @pl.when(jnp.logical_not(own))
        def _():
            arrived(kv.at[now], k_rs.at[13 + k])

        attend(now, chunk(i - 1)[2])

    stage(lambda cols: gather_values(oj * 4 + y2, cols))

    dealt(g_r, 2)
    gs[0:HD, :] = jnp.zeros((HD, 1024), BF)
    for b in range(4):
        cols = slice(b * 256, (b + 1) * 256)
        turned = g_r[b].astype(F32).T
        inv = 1.0 / jnp.sum(ls[:, cols], axis=0, keepdims=True)
        gt[:, b * 256 : b * 256 + 128] = turned[:HD] * inv[:, :128]
        gt[:, b * 256 + 128 : (b + 1) * 256] = turned[HD:] * inv[:, 128:]
        att[:, cols] = att[:, cols] * inv
    dqt[...] = jnp.zeros((HD, 1024), F32)

    def query_grad(ch, at, cols):
        dqt[:, cols] += mm(kvt[ch, 0:HD, :], ds[at, :, cols])

    def grads(ch, before, at):
        def score_grad(cols):
            query_grad(before, 1 - at, cols)
            shrink = jnp.exp2((tops[ch, 0:1, cols] - mx[0:1, cols]) * EXP2_SCALE)
            scaled = (gt[:, cols] * shrink).astype(BF)
            gs[HD:, cols] = scaled
            delta = jnp.sum(scaled.astype(F32) * att[:, cols], axis=0, keepdims=True)
            for r in range(2):
                rows = slice(r * 256, (r + 1) * 256)
                pg = mm(kv[ch, rows, :], gs[:, cols])
                ds[at, rows, cols] = (ex[ch, rows, cols].astype(F32) * (pg - delta)).astype(BF)

        stage(score_grad)
        dk = mm_t(qt[0:HD, :], ds[at]) * FACTOR
        dv = mm_t(gs[HD:, :], ex[ch])
        for zz in range(4):
            gk[zz, 0:HD, :] = dk[:, zz * 128 : (zz + 1) * 128]
            gk[zz, HD:, :] = dv[:, zz * 128 : (zz + 1) * 128]

    ds[1] = jnp.zeros((512, 1024), BF)

    at_kz = tuple((zh + k) % 4 for k in (2, 1, 3, 0))

    def turn(i):
        mine = (i == 2) | (i == 4) | (i == 5) | (i == 7)
        far = jnp.where(i < 4, jnp.where(i == 3, 3, jnp.where(i == 1, 1, 0)), 2)
        k = jnp.where(i == 4, 1, jnp.where(i == 5, 3, far))
        return mine, k, jnp.where(mine, j, oj) * 4 + (y + 2 + k) % 4

    @pl.loop(0, 8)
    def _(i):
        mine, k, now = turn(i)
        yy = (y + 2 + k) % 4
        grads(now, turn(jnp.maximum(i - 1, 0))[2], i % 2)

        @pl.when(jnp.logical_not(mine))
        def _():
            sb_s[k] = gk[...].astype(BF)
            send(sb_s.at[k], sb_r.at[k], ss.at[6], sb_rs.at[k], at_seq(y, zh, oj))

        @pl.when(mine)
        def _():
            arrived(sb_r.at[k], sb_rs.at[k])
            both = gk[...] + sb_r[k].astype(F32)

            @pl.when(k == 2)
            def _():
                tot[...] = both

            @pl.when(k != 2)
            def _():
                at = k - k // 3
                rs_s[at] = both.astype(BF)
                for n, zz in enumerate(at_kz):
                    send(
                        rs_s.at[at, zz], rs_r.at[at, zz], ss.at[11], r_rs.at[n],
                        at_seq(yy, zh, j),
                    )

    for n, zz in enumerate(at_kz):
        acc = tot[zz]
        arrived(rs_r.at[pl.ds(0, 3), 0], r_rs.at[n])
        for k in range(3):
            acc = acc + rs_r[k, zz].astype(F32)
        acc = acc.T
        if n < 3:
            k = (2, 1, 3)[n]
            zb_s[zz] = acc.astype(BF)
            send(zb_s.at[zz], hb.at[4 - k], ss.at[7], d_rs.at[8 - k], at_seq(y, zz, j))
        else:
            hb[0] = acc.astype(BF)

    stage(lambda cols: query_grad(j * 4 + y, 1, cols))
    for b in range(4):
        pair = [dqt[:, b * 256 + r * 128 : b * 256 + (r + 1) * 128] * FACTOR for r in range(2)]
        dq_s[b] = jnp.concatenate(pair, axis=0).T.astype(BF)

    far_first = (2, 3, 1, 0)

    def head_part(n, r, o):
        cols = pl.ds(pl.multiple_of((zh + o) % 4 * 128, 128), 128)
        return mm_t(hb[o], wp[(zh + far_first[n]) % 4, r * 512 : (r + 1) * 512, cols])

    for n in range(4):
        for r in range(2):
            pa[n, :, r * 512 : (r + 1) * 512] = head_part(n, r, 0)

    @pl.loop(0, 2)
    def _(i):
        o = 1 + 2 * i
        arrived(hb.at[o], d_rs.at[4 + o])
        for n in range(4):
            for r in range(2):
                pa[n, :, r * 512 : (r + 1) * 512] += head_part(n, r, o)

    arrived(hb.at[2], d_rs.at[6])

    def partial(n):
        for r in range(2):
            cols = slice(r * 512, (r + 1) * 512)
            part = pa[n, :, cols] + head_part(n, r, 2)
            pm[n, :, :, cols] = part.astype(BF).reshape(8, 16, 512)
        for i, (block, to) in enumerate((
            (col(x2, ol), col(x, ol)),
            (col(x1, ol), col(x1, zl)),
            (col(x3, ol), col(x3, zl)),
        )):
            send(pm.at[n, block], e1_r.at[n, i], ss.at[8], e_rs.at[n, (i + 1) // 2], (s, to))

    def combine(n):
        arrived(e1_r.at[n, 0], e_rs.at[n, 0])
        e2_s[n, 0] = (e1_r[n, 0].astype(F32) + pm[n, col(x2, zl)].astype(F32)).astype(BF)
        send(e2_s.at[n, 0], e2_r.at[n, 0], ss.at[9], e_rs.at[n, 2], (s, col(x2, zl)))
        arrived(e1_r.at[n, pl.ds(1, 2)], e_rs.at[n, 1])
        e2_s[n, 1] = (
            e1_r[n, 1].astype(F32) + e1_r[n, 2].astype(F32) + pm[n, col(x, ol)].astype(F32)
        ).astype(BF)
        send(e2_s.at[n, 1], e2_r.at[n, 1], ss.at[9], e_rs.at[n, 2], (s, col(x, ol)))
        for i, to in ((3, col(x1, zl)), (4, col(x3, zl))):
            send(pm.at[n, to], e1_r.at[n, i], ss.at[8], e_rs.at[n, 2], (s, to))

    def finish(n):
        acc = pm[n, c].astype(F32)
        arrived(e1_r.at[n, pl.ds(0, 4)], e_rs.at[n, 2])
        for i in range(2):
            acc = acc + e1_r[n, 3 + i].astype(F32) + e2_r[n, i].astype(F32)
        fs[n] = acc.astype(BF)
        feature_group(
            far_first[n],
            lambda o, cols: send(
                fs.at[n, :, cols], fo.at[s],
                ss.at[10], d_rs.at[4], (o, c),
            ),
        )

    for n in range(4):
        partial(n)
    for n in range(4):
        combine(n)
    deal(dq_s, dq_r, 3)
    finish(0)
    finish(1)
    finish(2)
    finish(3)
    dealt(dq_r, 3)
    for t in range(2):
        a = dq_r[2 * t].astype(F32)
        b = dq_r[2 * t + 1].astype(F32)
        tile = slice(t * 128, (t + 1) * 128)
        dq_out[0:128, tile], dq_out[128:256, tile] = halves(a, b)

    fo[s] = fs[3, :, my_cols]
    arrived(fo.at[pl.ds(0, 31)], d_rs.at[4])

    dm_out[...] = fo[...]

    for n, ref in enumerate((
        fo.at[pl.ds(0, 31)], kvl.at[pl.ds(0, 3)], kvl.at[pl.ds(0, 3)], kvl.at[pl.ds(0, 3)],
        mem.at[:, pl.ds(0, 7)], kv.at[pl.ds(0, 7)], sb_s, kvl.at[pl.ds(0, 3)],
        e1_r, e2_s, fo.at[pl.ds(0, 31)], rs_s, kvl.at[pl.ds(0, 3)],
    )):
        sent(ref, ss.at[n])


def local(memory, query, out_grad, w_key, w_value):
    dma = pltpu.SemaphoreType.DMA
    v = pltpu.VMEM
    dq, dm = pl.pallas_call(
        kernel,
        out_shape=(
            pltpu.VMEM((256, 256), BF),
            pltpu.VMEM((32, 16, 128), BF),
        ),
        in_specs=[pl.BlockSpec(memory_space=pl.ANY)] * 5,
        out_specs=(pl.BlockSpec(memory_space=pltpu.VMEM),) * 2,
        scratch_shapes=[
            v((32, 16, 128), BF),
            v((4096, 256), BF), v((4096, 256), BF), v((4, 1024, 512), BF),
            v((256, 256), BF), v((256, 256), BF),
            v((4, 8, 16, 1024), BF), v((4, 128, 128), BF),
            v((8, 512, 128), BF), v((8, 128, 512), BF),
            v((4, 128, 128), BF), v((4, 128, 128), BF), v((4, 128, 128), BF), v((4, 128, 128), BF),
            v((128, 1024), BF), v((HD, 1024), F32), v((128, 1024), BF),
            v((512, 1024), F32), v((8, 512, 1024), BF), v((2, 512, 1024), BF),
            v((8, 1024), F32), v((8, 8, 1024), F32), v((8, 1024), F32), v((8, 1024), F32), v((HD, 1024), F32),
            v((HD, 1024), F32), v((4, 128, 128), F32),
            v((4, 4, 128, 128), BF), v((4, 4, 128, 128), BF),
            v((3, 4, 128, 128), BF), v((3, 4, 128, 128), BF), v((4, 128, 128), F32),
            v((4, 128, 128), BF), v((4, 128, 128), BF), v((4, 128, 1024), F32),
            v((4, 128, 128), BF), v((4, 128, 128), BF),
            v((4, 8, 16, 1024), BF), v((4, 5, 16, 1024), BF),
            v((4, 2, 16, 1024), BF), v((4, 2, 16, 1024), BF),
            v((4, 16, 1024), BF), v((32, 16, 128), BF),
            dma((6,)), dma((13,)), dma((4,)), dma((4, 3)), dma((17,)), dma((4,)), dma((4,)),
            dma((8,)), dma((4, 3)),
        ],
        compiler_params=pltpu.CompilerParams(
            collective_id=0, has_side_effects=True, vmem_limit_bytes=60 * 1024 * 1024
        ),
    )(memory.reshape(32, 16, 128), query, out_grad, w_key, w_value)
    return pl.pallas_call(
        write_out,
        out_shape=(
            jax.ShapeDtypeStruct((256, 256), BF),
            jax.ShapeDtypeStruct((512, 128), BF),
        ),
        in_specs=[pl.BlockSpec(memory_space=pltpu.VMEM)] * 2,
        out_specs=(pl.BlockSpec(memory_space=pl.ANY),) * 2,
        scratch_shapes=[pltpu.SemaphoreType.DMA((2,))],
    )(
        pltpu.with_memory_space_constraint(dq, pltpu.VMEM),
        pltpu.with_memory_space_constraint(dm.reshape(512, 128), pltpu.VMEM),
    )


def write_out(dq_ref, dm_ref, dq_out, dm_out, sem):
    copies = [
        pltpu.make_async_copy(dq_ref, dq_out, sem.at[0]),
        pltpu.make_async_copy(dm_ref, dm_out, sem.at[1]),
    ]
    for copy in copies:
        copy.start()
    for copy in copies:
        copy.wait()


def solution(mesh):
    return jax.shard_map(
        local,
        mesh=mesh,
        in_specs=(
            P("col", "seq"),
            P("seq", "col"),
            P("seq", "col"),
            P(None, "col"),
            P(None, "col"),
        ),
        out_specs=(P("seq", "col"), P("col", "seq")),
        check_vma=False,
    )
```
